32 devices in a mesh: wide: 8 (over z, x), narrow: 4 (over y, core).
Axes of the slice: x: 2, y: 2, z: 4, core: 2. Of those that a mesh axis runs over, the one named last changes fastest.
Arguments:
- state: float32 [2, 2097152], P(None, ('wide', 'narrow')), may hold values from -6 to 6
- gates: float32 [8, 2, 128, 128], replicated, may hold values from -1 to 1, as said below
- gate_qubits: int32 [8, 7], replicated, may hold values from 7 to 15, as said below
- swap_order: int32 [9], replicated, may hold values from 7 to 15, as said below
Outputs:
- checkpoint: float32 [2, 2097152], P(None, ('wide', 'narrow'))
The draws below stay inside these ranges and needn't reach their ends.
Inputs may be any that keep to these rules, and one draw needn't show every extreme that they name: `gate_qubits`: each row names 7 different qubits. `swap_order`: each number of the range appears once. Each gates[g, 0] + i gates[g, 1] is a unitary matrix.
All inputs are finite; a program needn't handle non-finite values.
Results may differ from the reference program's by a relative error of at most 0.0003.
Values sent between devices are 32-bit elements; how exact they have to be, the bound alone decides.
A program may use at most 64 MiB of HBM per device.

```python
import math
import jax
import jax.numpy as jnp
from jax import lax

AMP_DEV = 65536
GATE_QUBITS = 7
LANE_QUBITS = 7
GATES = 8
GATE_DIM = 128
LOCAL_QUBITS = 16
NAMPS = 2097152
N_WIDE = 8
N_NARROW = 4


def orthonormal(matrix_pair):
    source_real = matrix_pair[0]
    source_imag = matrix_pair[1]
    extent = source_real.shape[0]

    def column_step(column, frames):
        frame_real, frame_imag = frames
        vector_real = lax.dynamic_index_in_dim(source_real, column, 1, keepdims=False)
        vector_imag = lax.dynamic_index_in_dim(source_imag, column, 1, keepdims=False)
        for repeat in range(2):
            weight_real = jnp.dot(frame_real.T, vector_real, precision=lax.Precision.HIGHEST) + jnp.dot(frame_imag.T, vector_imag, precision=lax.Precision.HIGHEST)
            weight_imag = jnp.dot(frame_real.T, vector_imag, precision=lax.Precision.HIGHEST) - jnp.dot(frame_imag.T, vector_real, precision=lax.Precision.HIGHEST)
            vector_real = vector_real - (jnp.dot(frame_real, weight_real, precision=lax.Precision.HIGHEST) - jnp.dot(frame_imag, weight_imag, precision=lax.Precision.HIGHEST))
            vector_imag = vector_imag - (jnp.dot(frame_real, weight_imag, precision=lax.Precision.HIGHEST) + jnp.dot(frame_imag, weight_real, precision=lax.Precision.HIGHEST))
        length = jnp.sqrt(jnp.sum(vector_real * vector_real + vector_imag * vector_imag))
        frame_real = lax.dynamic_update_index_in_dim(frame_real, vector_real / length, column, 1)
        frame_imag = lax.dynamic_update_index_in_dim(frame_imag, vector_imag / length, column, 1)
        return (frame_real, frame_imag)
    zeros_block = jnp.zeros((extent, extent), jnp.float32)
    frames = lax.fori_loop(0, extent, column_step, (zeros_block, zeros_block))
    return jnp.stack([frames[0], frames[1]])


def draw_gates(key, part):
    samples = jax.random.normal(jax.random.fold_in(key, 5), (GATES, 2, GATE_DIM, GATE_DIM), jnp.float32)
    return jax.vmap(orthonormal)(samples).astype(jnp.float32)


def draw_gate_qubits(key, part):
    subkeys = jax.random.split(jax.random.fold_in(key, 11), GATES)
    upper_count = LOCAL_QUBITS - LANE_QUBITS
    chosen = jax.vmap(lambda single: jax.random.permutation(single, upper_count)[:GATE_QUBITS])(subkeys)
    return (chosen + LANE_QUBITS).astype(jnp.int32)


def draw_swap_order(key, part):
    upper_count = LOCAL_QUBITS - LANE_QUBITS
    ordering = jax.random.permutation(jax.random.fold_in(key, 17), upper_count)
    return (ordering + LANE_QUBITS).astype(jnp.int32)


def level_of(key, dims, cuts, low, high):
    gain = 1.0
    for dim, blocks in cuts:
        steps = jax.random.uniform(jax.random.fold_in(jax.random.fold_in(key, 6), dim), (blocks,), jnp.float32, low / len(cuts), high / len(cuts))
        gain = gain * jnp.repeat(jnp.exp(steps), dims[dim] // blocks).reshape((-1,) + (1,) * (len(dims) - 1 - dim))
    return gain


def noise(key, shape, spread, most, shards=(), kind=jnp.bfloat16):
    array = jax.random.normal(key, shape, jnp.float32) * spread
    if len(shards) > 0:
        array = level_of(key, shape, shards, -0.22, 0.18) * array
    return jnp.clip(array, min=-most, max=most).astype(kind)


def setup_inputs(seed: int = 0) -> dict:
    keys = jax.random.split(jax.random.key(seed), 5)
    return {
        "state": noise(keys[0], (2, NAMPS), 1.0, 6.0, ((1, 32),), jnp.float32),
        "gates": draw_gates(jax.random.fold_in(keys[4], 71), 0),
        "gate_qubits": draw_gate_qubits(jax.random.fold_in(keys[4], 71), 0),
        "swap_order": draw_swap_order(jax.random.fold_in(keys[4], 71), 0),
    }


companding = 16.0
companding_norm = math.log(16.0 + math.sqrt(257.0))

def inverse_sinh(values):
    magnitude = jnp.abs(values)
    squared = magnitude * magnitude
    return jnp.sign(values) * jnp.log1p(magnitude + squared / (1.0 + jnp.sqrt(squared + 1.0)))

def shuffle_index(source, target, qubit_count):
    position = jnp.argsort(source).astype(jnp.int32)
    shifts = position[target].astype(jnp.int32)
    low_count = qubit_count // 2
    high_count = qubit_count - low_count
    low_values = jnp.arange(2 ** low_count, dtype=jnp.int32)
    high_values = jnp.arange(2 ** high_count, dtype=jnp.int32)
    low_bits = jnp.right_shift(low_values[:, None], jnp.arange(low_count, dtype=jnp.int32)[None, :]) & 1
    high_bits = jnp.right_shift(high_values[:, None], jnp.arange(high_count, dtype=jnp.int32)[None, :]) & 1
    low_part = lax.optimization_barrier(jnp.sum(jnp.left_shift(low_bits, shifts[None, :low_count]), axis=1)).astype(jnp.int32)
    high_part = lax.optimization_barrier(jnp.sum(jnp.left_shift(high_bits, shifts[None, low_count:]), axis=1)).astype(jnp.int32)
    return (high_part[:, None] + low_part[None, :]).reshape(-1).astype(jnp.int32)

def gate_order(chosen, qubit_count):
    ranking = jnp.arange(qubit_count, dtype=jnp.int32) + qubit_count
    ranking = ranking.at[chosen].set(jnp.arange(chosen.shape[0], dtype=jnp.int32))
    return jnp.argsort(ranking).astype(jnp.int32)

def top_order(chosen, qubit_count):
    ranking = jnp.arange(qubit_count, dtype=jnp.int32)
    ranking = ranking.at[chosen].set(qubit_count + jnp.arange(chosen.shape[0], dtype=jnp.int32))
    return jnp.argsort(ranking).astype(jnp.int32)

def gate_blocks(matrix):
    real_part = matrix[0]
    imag_part = matrix[1]
    return jnp.stack([jnp.stack([real_part, imag_part]), jnp.stack([-imag_part, real_part])])

def apply_local(values, matrix):
    shaped = values.reshape(2, -1, matrix.shape[-1])
    mixed = jnp.einsum('crb,cdab->dra', shaped, gate_blocks(matrix), precision=lax.Precision.HIGHEST)
    return mixed.reshape(values.shape)

def reference_gate(amplitudes, matrix, chosen):
    natural = jnp.arange(LOCAL_QUBITS, dtype=jnp.int32)
    layout = gate_order(chosen, LOCAL_QUBITS)
    arranged = jnp.take(amplitudes, shuffle_index(natural, layout, LOCAL_QUBITS), axis=2)
    mixed = apply_local(arranged, matrix)
    return jnp.take(mixed, shuffle_index(layout, natural, LOCAL_QUBITS), axis=2)

def reference_swap(amplitudes, chosen, group_count, first_axis):
    natural = jnp.arange(LOCAL_QUBITS, dtype=jnp.int32)
    layout = top_order(chosen, LOCAL_QUBITS)
    arranged = jnp.take(amplitudes, shuffle_index(natural, layout, LOCAL_QUBITS), axis=2)
    grid = arranged.reshape(2, N_WIDE, N_NARROW, group_count, AMP_DEV // group_count)
    grid = jnp.swapaxes(grid, first_axis, 3)
    arranged = grid.reshape(2, N_WIDE * N_NARROW, AMP_DEV)
    return jnp.take(arranged, shuffle_index(layout, natural, LOCAL_QUBITS), axis=2)

def reference(state, gates, gate_qubits, swap_order):
    wide_bits = N_WIDE.bit_length() - 1
    narrow_bits = N_NARROW.bit_length() - 1
    upper_count = LOCAL_QUBITS - LANE_QUBITS
    amplitudes = state.reshape(2, N_WIDE * N_NARROW, AMP_DEV)
    for number in range(3):
        amplitudes = reference_gate(amplitudes, gates[number], gate_qubits[number])
    amplitudes = reference_swap(amplitudes, swap_order[upper_count - wide_bits:], N_WIDE, 1)
    for number in range(3, 6):
        amplitudes = reference_gate(amplitudes, gates[number], gate_qubits[number])
    amplitudes = reference_swap(amplitudes, swap_order[:narrow_bits], N_NARROW, 2)
    for number in range(6, 8):
        amplitudes = reference_gate(amplitudes, gates[number], gate_qubits[number])
    final = amplitudes.reshape(2, -1)
    highest = jnp.max(final)
    lowest = jnp.min(final)
    middle = (highest + lowest) * 0.5
    halfwidth = (highest - lowest) * 0.5 + 1e-06
    return inverse_sinh(companding * (final - middle) / halfwidth) / companding_norm
```

```python
import functools
import math

import jax
import jax.numpy as jnp
from jax import lax
from jax.experimental import pallas as pl
from jax.experimental.pallas import tpu as pltpu
from jax.sharding import PartitionSpec as P

LANE_QUBITS = 7
LANES = 2**LANE_QUBITS
CHUNKS = 2

companding = 16.0
companding_norm = math.log(16.0 + math.sqrt(257.0))

MESH = pl.DeviceIdType.MESH


def plain_kernel(
    n_wide,
    n_narrow,
    upper,
    gate_bits,
    stages,
    qubits_hbm,
    swap_hbm,
    state_ref,
    gates_ref,
    out_ref,
    qubits_ref,
    swap_ref,
    state_v,
    gates_v,
    perms,
    mats,
    wide_out,
    wide_in,
    narrow_out,
    narrow_in,
    ext_out,
    ext_in,
    local_sem,
    gate_sem,
    wide_send,
    wide_recv,
    narrow_send,
    narrow_recv,
    ext_send,
    ext_recv,
):
    rows = 2**upper
    gate_dim = 2**gate_bits
    rest = rows // gate_dim
    wide_bits = n_wide.bit_length() - 1
    narrow_bits = n_narrow.bit_length() - 1
    wide_me = lax.axis_index("wide")
    narrow_me = lax.axis_index("narrow")
    half = LANES // 2

    qubits_copy = pltpu.make_async_copy(qubits_hbm, qubits_ref, local_sem.at[1])
    qubits_copy.start()
    swap_copy = pltpu.make_async_copy(swap_hbm, swap_ref, local_sem.at[2])
    swap_copy.start()
    state_copy = pltpu.make_async_copy(state_ref, state_v, local_sem.at[0])
    state_copy.start()
    gate_copies = []
    for number in range(gates_v.shape[0]):
        copy = pltpu.make_async_copy(
            gates_ref.at[number], gates_v.at[number], gate_sem.at[number]
        )
        copy.start()
        gate_copies.append(copy)

    barrier = pltpu.get_barrier_semaphore()
    devices = n_wide * n_narrow
    flat_me = wide_me * n_narrow + narrow_me

    def device_at(apart):
        other = lax.rem(flat_me + apart, devices)
        return (lax.div(other, n_narrow), lax.rem(other, n_narrow))

    def for_others(step):
        if devices <= 64:
            for apart in range(1, devices):
                step(apart)
        else:
            lax.fori_loop(1, devices, lambda apart, _: step(apart), None)

    def greet(apart):
        pl.semaphore_signal(barrier, inc=1, device_id=device_at(apart), device_id_type=MESH)

    for_others(greet)
    qubits_copy.wait()
    swap_copy.wait()

    def gate_layout(number):
        masks = [jnp.int32(1) << (qubits_ref[number, k] - LANE_QUBITS) for k in range(gate_bits)]
        left = jnp.int32(rows - 1)
        for mask in masks:
            left = left - mask
        for _ in range(upper - gate_bits):
            low = left & (-left)
            masks.append(low)
            left = left - low
        return masks

    def swap_layout(order):
        return [jnp.int32(1) << (swap_ref[k] - LANE_QUBITS) for k in order]

    natural = [jnp.int32(1 << k) for k in range(upper)]
    wide_layout = swap_layout(range(upper))
    narrow_layout = swap_layout(list(range(narrow_bits, upper)) + list(range(narrow_bits)))

    column = lax.broadcasted_iota(jnp.int32, (1, rows), 1)
    row = lax.broadcasted_iota(jnp.int32, (rows, rows), 0)

    def make_perm(slot, source, target):
        index = jnp.zeros((1, rows), jnp.int32)
        for k in range(upper):
            index = index + jnp.where((column & (1 << k)) != 0, source[k], 0)
        goal = jnp.zeros((1, rows), jnp.int32)
        for k in range(upper):
            goal = goal + jnp.where((index & target[k]) != 0, 1 << k, 0)
        perms[slot] = (row == goal).astype(jnp.float32).astype(jnp.bfloat16)

    def make_matrix(number):
        gate_copies[number].wait()
        whole = jnp.concatenate([gates_v[number, 0], gates_v[number, 1]], axis=1)
        high = whole.astype(jnp.bfloat16)
        low = (whole - high.astype(jnp.float32)).astype(jnp.bfloat16)
        mats[number, :gate_dim] = high
        mats[number, gate_dim:] = low

    sign = jnp.where(lax.broadcasted_iota(jnp.int32, (1, LANES), 1) < half, -1.0, 1.0)

    def permuted(values, slot):
        high = values.astype(jnp.bfloat16)
        low = (values - high.astype(jnp.float32)).astype(jnp.bfloat16)
        both = jnp.concatenate([high, low], axis=1)
        moved = jnp.dot(perms[slot], both, preferred_element_type=jnp.float32)
        return moved[:, :LANES], moved[:, LANES:]

    def gate(values, slot, number):
        both = jnp.concatenate(permuted(values, slot), axis=1)
        blocks = []
        for k in range(rest):
            part = both[k * gate_dim : (k + 1) * gate_dim]
            turned = jnp.concatenate(
                [
                    pltpu.roll(part[:, :LANES], half, 1) * sign,
                    pltpu.roll(part[:, LANES:], half, 1) * sign,
                ],
                axis=1,
            )
            whole = jnp.concatenate([part, turned], axis=0).astype(jnp.bfloat16)
            mixed = jnp.dot(mats[number], whole, preferred_element_type=jnp.float32)
            blocks.append(
                mixed[:gate_dim, :LANES]
                + (mixed[gate_dim:, :LANES] + mixed[:gate_dim, LANES:])
            )
        return jnp.concatenate(blocks, axis=0)

    def moved(values, slot):
        high, low = permuted(values, slot)
        return high + low

    def wide_copy(chunk, apart):
        other = lax.rem(wide_me + apart, n_wide)
        return pltpu.make_async_remote_copy(
            src_ref=wide_out.at[chunk, other],
            dst_ref=wide_in.at[chunk, wide_me],
            send_sem=wide_send.at[chunk, apart - 1],
            recv_sem=wide_recv.at[chunk, apart - 1],
            device_id=(other, narrow_me),
            device_id_type=MESH,
        )

    def narrow_copy(chunk, apart):
        other = lax.rem(narrow_me + apart, n_narrow)
        return pltpu.make_async_remote_copy(
            src_ref=narrow_out.at[chunk, other],
            dst_ref=narrow_in.at[chunk, narrow_me],
            send_sem=narrow_send.at[chunk, apart - 1],
            recv_sem=narrow_recv.at[chunk, apart - 1],
            device_id=(wide_me, other),
            device_id_type=MESH,
        )

    slot = 0
    plan = []
    for numbers, leave in zip(stages, (wide_layout, narrow_layout, natural)):
        plan.append((slot, numbers, leave))
        slot += len(numbers) + 1

    def prepare(stage, layout):
        start, numbers, leave = plan[stage]
        for k, number in enumerate(numbers):
            target = gate_layout(number)
            make_perm(start + k, layout, target)
            make_matrix(number)
            layout = target
        make_perm(start + len(numbers), layout, leave)

    def run(values, stage):
        start, numbers, _ = plan[stage]
        for k, number in enumerate(numbers):
            values = gate(values, start + k, number)
        return moved(values, start + len(numbers))

    prepare(0, natural)
    state_copy.wait()
    real = state_v[pl.ds(0, rows, stride=2), :]
    imag = state_v[pl.ds(1, rows, stride=2), :]
    first_half = lax.broadcasted_iota(jnp.int32, (1, LANES), 1) < half
    pieces = (
        jnp.where(first_half, real, pltpu.roll(imag, half, 1)),
        jnp.where(first_half, pltpu.roll(real, half, 1), imag),
    )
    for chunk in range(CHUNKS):
        values = run(pieces[chunk], 0)
        wide_out[chunk] = values.reshape(n_wide, rows // n_wide, LANES)
        if chunk == 0:
            pl.semaphore_wait(barrier, devices - 1)
        for apart in range(1, n_wide):
            wide_copy(chunk, apart).start()
        wide_in[chunk, wide_me] = wide_out[chunk, wide_me]

    prepare(1, wide_layout)
    prepare(2, narrow_layout)
    for chunk in range(CHUNKS):
        for apart in range(1, n_wide):
            wide_copy(chunk, apart).wait_recv()
        values = run(wide_in[chunk].reshape(rows, LANES), 1)
        narrow_out[chunk] = values.reshape(n_narrow, rows // n_narrow, LANES)
        for apart in range(1, n_narrow):
            narrow_copy(chunk, apart).start()
        narrow_in[chunk, narrow_me] = narrow_out[chunk, narrow_me]

    results = []
    for chunk in range(CHUNKS):
        for apart in range(1, n_narrow):
            narrow_copy(chunk, apart).wait_recv()
        results.append(run(narrow_in[chunk].reshape(rows, LANES), 2))

    high = jnp.maximum(results[0], results[1]).max(axis=0, keepdims=True)
    low = -jnp.minimum(results[0], results[1]).min(axis=0, keepdims=True)
    high = jnp.maximum(high, pltpu.roll(high, half, 1))
    low = jnp.maximum(low, pltpu.roll(low, half, 1))
    ext_out[...] = jnp.where(first_half, high, low)

    def ext_copy(apart):
        return pltpu.make_async_remote_copy(
            src_ref=ext_out,
            dst_ref=ext_in.at[apart - 1],
            send_sem=ext_send.at[apart - 1],
            recv_sem=ext_recv.at[apart - 1],
            device_id=device_at(apart),
            device_id_type=MESH,
        )

    for_others(lambda apart: ext_copy(apart).start())
    state_v[:rows] = jnp.where(first_half, results[0], pltpu.roll(results[1], half, 1))
    state_v[rows:] = jnp.where(first_half, pltpu.roll(results[0], half, 1), results[1])
    for chunk in range(CHUNKS):
        for apart in range(1, n_wide):
            wide_copy(chunk, apart).wait_send()
        for apart in range(1, n_narrow):
            narrow_copy(chunk, apart).wait_send()
    for_others(lambda apart: ext_copy(apart).wait_recv())
    total = jnp.maximum(ext_out[...], ext_in[...].max(axis=0))
    highest = jnp.max(jnp.where(first_half, total, -jnp.inf), axis=1, keepdims=True)
    lowest = -jnp.max(jnp.where(first_half, -jnp.inf, total), axis=1, keepdims=True)
    middle = (highest + lowest) * 0.5
    halfwidth = (highest - lowest) * 0.5 + 1e-06
    scale = companding / halfwidth
    for plane in range(2):
        values = (state_v[plane * rows : (plane + 1) * rows] - middle) * scale
        magnitude = jnp.abs(values)
        squared = magnitude * magnitude + 1.0
        grown = jnp.log(magnitude + squared * lax.rsqrt(squared)) * (1.0 / companding_norm)
        out_ref[pl.ds(plane, rows, stride=2), :] = jnp.where(values < 0, -grown, grown)
    for_others(lambda apart: ext_copy(apart).wait_send())


def plain_local(state, gates, gate_qubits, swap_order):
    n_wide = lax.axis_size("wide")
    n_narrow = lax.axis_size("narrow")
    upper = state.shape[1].bit_length() - 1 - LANE_QUBITS
    rows = 2**upper
    gate_count, gate_bits = gate_qubits.shape
    gate_dim = 2**gate_bits
    stages = (range(3), range(3, 6), range(6, gate_count))
    dma = pltpu.SemaphoreType.DMA
    woven = state.reshape(2, rows, LANES).transpose(1, 0, 2).reshape(2 * rows, LANES)
    final = pl.pallas_call(
        functools.partial(plain_kernel, n_wide, n_narrow, upper, gate_bits, stages),
        out_shape=jax.ShapeDtypeStruct((2 * rows, LANES), jnp.float32),
        in_specs=[pl.BlockSpec(memory_space=pltpu.HBM)] * 4,
        out_specs=pl.BlockSpec(memory_space=pltpu.VMEM),
        scratch_shapes=[
            pltpu.SMEM(gate_qubits.shape, jnp.int32),
            pltpu.SMEM(swap_order.shape, jnp.int32),
            pltpu.VMEM((2 * rows, LANES), jnp.float32),
            pltpu.VMEM(gates.shape, jnp.float32),
            pltpu.VMEM((gate_count + 3, rows, rows), jnp.bfloat16),
            pltpu.VMEM((gate_count, 2 * gate_dim, 2 * gate_dim), jnp.bfloat16),
            pltpu.VMEM((CHUNKS, n_wide, rows // n_wide, LANES), jnp.float32),
            pltpu.VMEM((CHUNKS, n_wide, rows // n_wide, LANES), jnp.float32),
            pltpu.VMEM((CHUNKS, n_narrow, rows // n_narrow, LANES), jnp.float32),
            pltpu.VMEM((CHUNKS, n_narrow, rows // n_narrow, LANES), jnp.float32),
            pltpu.VMEM((1, LANES), jnp.float32),
            pltpu.VMEM((n_wide * n_narrow - 1, 1, LANES), jnp.float32),
            dma((3,)),
            dma((gate_count,)),
            dma((CHUNKS, n_wide - 1)),
            dma((CHUNKS, n_wide - 1)),
            dma((CHUNKS, n_narrow - 1)),
            dma((CHUNKS, n_narrow - 1)),
            dma((n_wide * n_narrow - 1,)),
            dma((n_wide * n_narrow - 1,)),
        ],
        compiler_params=pltpu.CompilerParams(
            collective_id=0, has_side_effects=True, vmem_limit_bytes=67043328
        ),
        name="plain_gate_layers",
    )(gate_qubits, swap_order, woven, gates)
    return final.reshape(rows, 2, LANES).transpose(1, 0, 2).reshape(state.shape)


SIZES = (32, 32, 32, 32)
GROUPS = ((0,), (1, 2, 3))


def kernel(
    n_wide,
    n_narrow,
    upper,
    gate_bits,
    stages,
    sizes,
    groups,
    qubits_hbm,
    swap_hbm,
    state_ref,
    gates_ref,
    out_ref,
    middle_ref,
    scale_ref,
    qubits_ref,
    swap_ref,
    state_v,
    gates_v,
    perms,
    mats,
    turned,
    wide_out,
    wide_in,
    narrow_out,
    narrow_in,
    final,
    ext_out,
    ext_in,
    local_sem,
    gate_sem,
    wide_send,
    wide_recv,
    narrow_send,
    narrow_recv,
    ext_send,
    ext_recv,
):
    rows = 2**upper
    gate_dim = 2**gate_bits
    rest = rows // gate_dim
    tiles = rows // LANES
    narrow_bits = n_narrow.bit_length() - 1
    wide_me = lax.axis_index("wide")
    narrow_me = lax.axis_index("narrow")
    half = LANES // 2
    chunks = range(len(sizes))
    starts = [sum(sizes[:k]) for k in chunks]
    devices = n_wide * n_narrow
    flat_me = wide_me * n_narrow + narrow_me
    f32, bf16 = jnp.float32, jnp.bfloat16

    state_copy = pltpu.make_async_copy(state_ref, state_v, local_sem.at[0])
    state_copy.start()
    qubits_copy = pltpu.make_async_copy(qubits_hbm, qubits_ref, local_sem.at[1])
    qubits_copy.start()
    swap_copy = pltpu.make_async_copy(swap_hbm, swap_ref, local_sem.at[2])
    swap_copy.start()
    gate_copies = []
    for number in range(gates_v.shape[0]):
        copy = pltpu.make_async_copy(
            gates_ref.at[number], gates_v.at[number], gate_sem.at[number]
        )
        copy.start()
        gate_copies.append(copy)

    barrier = pltpu.get_barrier_semaphore()

    def device_at(apart):
        other = lax.rem(flat_me + apart, devices)
        return (lax.div(other, n_narrow), lax.rem(other, n_narrow))

    for apart in range(1, devices):
        pl.semaphore_signal(barrier, inc=1, device_id=device_at(apart), device_id_type=MESH)

    def fenced(step):
        pl.when(flat_me >= 0)(step)

    def gate_layout(number):
        masks = [jnp.int32(1) << (qubits_ref[number, k] - LANE_QUBITS) for k in range(gate_bits)]
        left = jnp.int32(rows - 1)
        for mask in masks:
            left = left - mask
        for _ in range(upper - gate_bits):
            low = left & (-left)
            masks.append(low)
            left = left - low
        return masks

    def swap_layout(order):
        return [jnp.int32(1) << (swap_ref[k] - LANE_QUBITS) for k in order]

    natural = [jnp.int32(1 << k) for k in range(upper)]
    column = lax.broadcasted_iota(jnp.int32, (1, rows), 1)
    row = lax.broadcasted_iota(jnp.int32, (rows, rows), 0)
    first_half = lax.broadcasted_iota(jnp.int32, (1, LANES), 1) < half

    def make_perm(slot, source, target):
        index = jnp.zeros((1, rows), jnp.int32)
        for k in range(upper):
            index = index + jnp.where((column & (1 << k)) != 0, target[k], 0)
        place = jnp.zeros((1, rows), jnp.int32)
        for k in range(upper):
            place = place + jnp.where((index & source[k]) != 0, 1 << k, 0)
        perms[slot] = (row == place).astype(f32).astype(bf16)

    def split(values):
        high = values.astype(bf16)
        return high, (values - high.astype(f32)).astype(bf16)

    def make_matrix(number):
        gate_copies[number].wait()
        real = gates_v[number, 0].T
        imag = gates_v[number, 1].T
        whole = jnp.concatenate(
            [jnp.concatenate([real, imag], axis=1), jnp.concatenate([-imag, real], axis=1)],
            axis=0,
        )
        high, low = split(whole)
        mats[number, : 2 * gate_dim] = high
        mats[number, 2 * gate_dim : 4 * gate_dim] = high
        mats[number, 4 * gate_dim :] = low

    def moved(parts, slot):
        return jnp.dot(parts, perms[slot], preferred_element_type=f32)

    def gate(parts, slot, number):
        count = parts.shape[0] // 4
        parts = moved(parts, slot).astype(bf16)

        def side(first):
            return jnp.concatenate(
                [
                    jnp.concatenate(
                        [
                            parts[first : first + count, k * gate_dim : (k + 1) * gate_dim],
                            parts[first + count : first + 2 * count, k * gate_dim : (k + 1) * gate_dim],
                        ],
                        axis=1,
                    )
                    for k in range(rest)
                ],
                axis=0,
            )

        high, low = side(0), side(2 * count)
        mixed = jnp.dot(
            jnp.concatenate([high, low, high], axis=1), mats[number], preferred_element_type=f32
        )
        return jnp.concatenate(
            [
                jnp.concatenate(
                    [
                        part[k * count : (k + 1) * count, plane * gate_dim : (plane + 1) * gate_dim]
                        for k in range(rest)
                    ],
                    axis=1,
                )
                for part in split(mixed)
                for plane in range(2)
            ],
            axis=0,
        )

    slot = 0
    plan = []
    for numbers in stages:
        plan.append((slot, numbers))
        slot += len(numbers) + 1

    def prepare(stage, layout, leave):
        start, numbers = plan[stage]
        for k, number in enumerate(numbers):
            target = gate_layout(number)
            make_perm(start + k, layout, target)
            make_matrix(number)
            layout = target
        make_perm(start + len(numbers), layout, leave)

    def run(parts, stage):
        start, numbers = plan[stage]
        for k, number in enumerate(numbers):
            parts = gate(parts, start + k, number)
        both = moved(parts, start + len(numbers))
        count = both.shape[0] // 2
        return both[:count] + both[count:]

    def wide_copy(chunk, apart):
        other = lax.rem(wide_me + apart, n_wide)
        part = pl.ds(starts[chunk], sizes[chunk])
        return pltpu.make_async_remote_copy(
            src_ref=wide_out.at[other, part],
            dst_ref=wide_in.at[wide_me, part],
            send_sem=wide_send.at[chunk, apart - 1],
            recv_sem=wide_recv.at[chunk, apart - 1],
            device_id=(other, narrow_me),
            device_id_type=MESH,
        )

    def narrow_copy(chunk, apart):
        other = lax.rem(narrow_me + apart, n_narrow)
        part = pl.ds(2 * starts[chunk], 2 * sizes[chunk])
        return pltpu.make_async_remote_copy(
            src_ref=narrow_out.at[other, part],
            dst_ref=narrow_in.at[narrow_me, part],
            send_sem=narrow_send.at[chunk, apart - 1],
            recv_sem=narrow_recv.at[chunk, apart - 1],
            device_id=(wide_me, other),
            device_id_type=MESH,
        )

    def ext_copy(apart):
        return pltpu.make_async_remote_copy(
            src_ref=ext_out,
            dst_ref=ext_in.at[apart - 1],
            send_sem=ext_send.at[apart - 1],
            recv_sem=ext_recv.at[apart - 1],
            device_id=device_at(apart),
            device_id_type=MESH,
        )

    def first_stage(group):
        first, count = starts[group[0]], sum(sizes[k] for k in group)
        parts = jnp.concatenate(
            [turned[k, first : first + count] for k in range(4)], axis=0
        )
        both = run(parts, 0)
        real, imag = both[:count], both[count:]
        for m in range(tiles):
            re, im = real[:, m * LANES : (m + 1) * LANES], imag[:, m * LANES : (m + 1) * LANES]
            wide_out[2 * m, first : first + count] = jnp.where(
                first_half, re, pltpu.roll(im, half, 1)
            )
            wide_out[2 * m + 1, first : first + count] = jnp.where(
                first_half, pltpu.roll(re, half, 1), im
            )

    def first_send(group):
        first, count = starts[group[0]], sum(sizes[k] for k in group)
        for chunk in group:
            for apart in range(1, n_wide):
                wide_copy(chunk, apart).start()
        part = pl.ds(first, count)
        wide_in[wide_me, part] = wide_out[wide_me, part]

    def second_stage(chunk):
        first, count = starts[chunk], sizes[chunk]
        for apart in range(1, n_wide):
            wide_copy(chunk, apart).wait_recv()
        real, imag = [], []
        for m in range(tiles):
            left = wide_in[2 * m, first : first + count]
            right = wide_in[2 * m + 1, first : first + count]
            real.append(jnp.where(first_half, left, pltpu.roll(right, half, 1)))
            imag.append(jnp.where(first_half, pltpu.roll(left, half, 1), right))
        whole = jnp.concatenate(
            [jnp.concatenate(real, axis=1), jnp.concatenate(imag, axis=1)], axis=0
        )
        both = run(jnp.concatenate(split(whole), axis=0), 1)
        width = rows // n_narrow
        for m in range(n_narrow):
            narrow_out[m, 2 * first : 2 * (first + count)] = both[:, m * width : (m + 1) * width]

    def second_send(chunk):
        for apart in range(1, n_narrow):
            narrow_copy(chunk, apart).start()
        part = pl.ds(2 * starts[chunk], 2 * sizes[chunk])
        narrow_in[narrow_me, part] = narrow_out[narrow_me, part]

    def third_stage(chunk):
        first, count = starts[chunk], sizes[chunk]
        for apart in range(1, n_narrow):
            narrow_copy(chunk, apart).wait_recv()
        whole = jnp.concatenate(
            [narrow_in[m, 2 * first : 2 * (first + count)] for m in range(n_narrow)], axis=1
        )
        both = run(jnp.concatenate(split(whole), axis=0), 2)
        final[0, first : first + count] = both[:count]
        final[1, first : first + count] = both[count:]

    qubits_copy.wait()
    prepare_first = functools.partial(prepare, 0, natural)
    swap_copy.wait()
    wide_layout = swap_layout(range(upper))
    narrow_layout = swap_layout(list(range(narrow_bits, upper)) + list(range(narrow_bits)))
    prepare_first(wide_layout)
    state_copy.wait()
    for plane in range(2):
        high, low = split(state_v[pl.ds(plane, rows, stride=2), :].T)
        turned[plane] = high
        turned[2 + plane] = low
    first_stage(groups[0])
    pl.semaphore_wait(barrier, devices - 1)
    first_send(groups[0])

    for group in groups[1:]:

        @fenced
        def _(group=group):
            first_stage(group)
            first_send(group)

    @fenced
    def _():
        prepare(1, wide_layout, narrow_layout)
        prepare(2, narrow_layout, natural)

    last = len(sizes) - 1
    for chunk in chunks:

        @fenced
        def _(chunk=chunk):
            second_stage(chunk)
            second_send(chunk)

        if chunk > 0:

            @fenced
            def _(chunk=chunk):
                third_stage(chunk - 1)

    @fenced
    def _():
        third_stage(last)
        whole = final[...]
        high, low = whole.max(axis=0), -whole.min(axis=0)
        high, low = high.max(axis=0, keepdims=True), low.max(axis=0, keepdims=True)
        for k, value in enumerate((high, low)):
            value = functools.reduce(
                jnp.maximum, [value[:, m * LANES : (m + 1) * LANES] for m in range(tiles)]
            )
            ext_out[k : k + 1] = value
        for apart in range(1, devices):
            ext_copy(apart).start()

    @fenced
    def _():
        for plane in range(2):
            out_ref[pl.ds(plane, rows, stride=2), :] = final[plane].T
        for chunk in chunks:
            for apart in range(1, n_wide):
                wide_copy(chunk, apart).wait_send()
            for apart in range(1, n_narrow):
                narrow_copy(chunk, apart).wait_send()

    for apart in range(1, devices):
        ext_copy(apart).wait_recv()
    total = jnp.maximum(ext_out[...], ext_in[...].max(axis=0))
    total = jnp.max(total, axis=1, keepdims=True)
    highest, lowest = total[0:1], -total[1:2]
    middle = (highest + lowest) * 0.5
    halfwidth = (highest - lowest) * 0.5 + 1e-06
    middle_ref[...] = jnp.broadcast_to(middle, (1, LANES))
    scale_ref[...] = jnp.broadcast_to(companding / halfwidth, (1, LANES))
    for apart in range(1, devices):
        ext_copy(apart).wait_send()


def local(state, gates, gate_qubits, swap_order):
    n_wide = lax.axis_size("wide")
    n_narrow = lax.axis_size("narrow")
    upper = state.shape[1].bit_length() - 1 - LANE_QUBITS
    rows = 2**upper
    gate_count, gate_bits = gate_qubits.shape
    gate_dim = 2**gate_bits
    devices = n_wide * n_narrow
    if 2 * rows != n_wide * LANES or rows != n_narrow * LANES or gate_dim != LANES:
        return plain_local(state, gates, gate_qubits, swap_order)
    stages = (range(3), range(3, 6), range(6, gate_count))
    dma = pltpu.SemaphoreType.DMA
    bf16, f32 = jnp.bfloat16, jnp.float32
    chunks = len(SIZES)
    woven = state.reshape(2, rows, LANES).transpose(1, 0, 2).reshape(2 * rows, LANES)
    held = [pltpu.with_memory_space_constraint(x, pltpu.HBM) for x in (gate_qubits, swap_order, woven, gates)]
    final, middle, scale = pl.pallas_call(
        functools.partial(kernel, n_wide, n_narrow, upper, gate_bits, stages, SIZES, GROUPS),
        out_shape=(
            pltpu.VMEM((2 * rows, LANES), f32),
            pltpu.VMEM((1, LANES), f32),
            pltpu.VMEM((1, LANES), f32),
        ),
        in_specs=[pl.BlockSpec(memory_space=pltpu.HBM)] * 4,
        out_specs=[pl.BlockSpec(memory_space=pltpu.VMEM)] * 3,
        scratch_shapes=[
            pltpu.SMEM(gate_qubits.shape, jnp.int32),
            pltpu.SMEM(swap_order.shape, jnp.int32),
            pltpu.VMEM((2 * rows, LANES), f32),
            pltpu.VMEM(gates.shape, f32),
            pltpu.VMEM((gate_count + 3, rows, rows), bf16),
            pltpu.VMEM((gate_count, 6 * gate_dim, 2 * gate_dim), bf16),
            pltpu.VMEM((4, LANES, rows), bf16),
            pltpu.VMEM((n_wide, LANES, LANES), f32),
            pltpu.VMEM((n_wide, LANES, LANES), f32),
            pltpu.VMEM((n_narrow, 2 * LANES, LANES), f32),
            pltpu.VMEM((n_narrow, 2 * LANES, LANES), f32),
            pltpu.VMEM((2, LANES, rows), f32),
            pltpu.VMEM((2, LANES), f32),
            pltpu.VMEM((devices - 1, 2, LANES), f32),
            dma((3,)),
            dma((gate_count,)),
            dma((chunks, n_wide - 1)),
            dma((chunks, n_wide - 1)),
            dma((chunks, n_narrow - 1)),
            dma((chunks, n_narrow - 1)),
            dma((devices - 1,)),
            dma((devices - 1,)),
        ],
        compiler_params=pltpu.CompilerParams(
            collective_id=0, has_side_effects=True, vmem_limit_bytes=40000000
        ),
        name="gate_layers",
    )(*held)
    values = (final - middle) * scale
    magnitude = jnp.abs(values)
    squared = magnitude * magnitude + 1.0
    grown = jnp.log(magnitude + squared * lax.rsqrt(squared)) * (1.0 / companding_norm)
    final = jnp.where(values < 0, -grown, grown)
    return final.reshape(rows, 2, LANES).transpose(1, 0, 2).reshape(state.shape)


def solution(mesh):
    in_specs = (P(None, ("wide", "narrow")), P(), P(), P())
    out_specs = P(None, ("wide", "narrow"))
    return jax.shard_map(local, mesh=mesh, in_specs=in_specs, out_specs=out_specs, check_vma=False)
```

```python
import functools
import math

import jax
import jax.numpy as jnp
from jax import lax
from jax.experimental import pallas as pl
from jax.experimental.pallas import tpu as pltpu
from jax.sharding import PartitionSpec as P

LANE_QUBITS = 7
LANES = 2**LANE_QUBITS
CHUNKS = 2

companding = 16.0
companding_norm = math.log(16.0 + math.sqrt(257.0))

MESH = pl.DeviceIdType.MESH


def plain_kernel(
    n_wide,
    n_narrow,
    upper,
    gate_bits,
    stages,
    qubits_hbm,
    swap_hbm,
    state_ref,
    gates_ref,
    out_ref,
    qubits_ref,
    swap_ref,
    state_v,
    gates_v,
    perms,
    mats,
    wide_out,
    wide_in,
    narrow_out,
    narrow_in,
    ext_out,
    ext_in,
    local_sem,
    gate_sem,
    wide_send,
    wide_recv,
    narrow_send,
    narrow_recv,
    ext_send,
    ext_recv,
):
    rows = 2**upper
    gate_dim = 2**gate_bits
    rest = rows // gate_dim
    wide_bits = n_wide.bit_length() - 1
    narrow_bits = n_narrow.bit_length() - 1
    wide_me = lax.axis_index("wide")
    narrow_me = lax.axis_index("narrow")
    half = LANES // 2

    qubits_copy = pltpu.make_async_copy(qubits_hbm, qubits_ref, local_sem.at[1])
    qubits_copy.start()
    swap_copy = pltpu.make_async_copy(swap_hbm, swap_ref, local_sem.at[2])
    swap_copy.start()
    state_copy = pltpu.make_async_copy(state_ref, state_v, local_sem.at[0])
    state_copy.start()
    gate_copies = []
    for number in range(gates_v.shape[0]):
        copy = pltpu.make_async_copy(
            gates_ref.at[number], gates_v.at[number], gate_sem.at[number]
        )
        copy.start()
        gate_copies.append(copy)

    barrier = pltpu.get_barrier_semaphore()
    devices = n_wide * n_narrow
    flat_me = wide_me * n_narrow + narrow_me

    def device_at(apart):
        other = lax.rem(flat_me + apart, devices)
        return (lax.div(other, n_narrow), lax.rem(other, n_narrow))

    def for_others(step):
        if devices <= 64:
            for apart in range(1, devices):
                step(apart)
        else:
            lax.fori_loop(1, devices, lambda apart, _: step(apart), None)

    def greet(apart):
        pl.semaphore_signal(barrier, inc=1, device_id=device_at(apart), device_id_type=MESH)

    for_others(greet)
    qubits_copy.wait()
    swap_copy.wait()

    def gate_layout(number):
        masks = [jnp.int32(1) << (qubits_ref[number, k] - LANE_QUBITS) for k in range(gate_bits)]
        left = jnp.int32(rows - 1)
        for mask in masks:
            left = left - mask
        for _ in range(upper - gate_bits):
            low = left & (-left)
            masks.append(low)
            left = left - low
        return masks

    def swap_layout(order):
        return [jnp.int32(1) << (swap_ref[k] - LANE_QUBITS) for k in order]

    natural = [jnp.int32(1 << k) for k in range(upper)]
    wide_layout = swap_layout(range(upper))
    narrow_layout = swap_layout(list(range(narrow_bits, upper)) + list(range(narrow_bits)))

    column = lax.broadcasted_iota(jnp.int32, (1, rows), 1)
    row = lax.broadcasted_iota(jnp.int32, (rows, rows), 0)

    def make_perm(slot, source, target):
        index = jnp.zeros((1, rows), jnp.int32)
        for k in range(upper):
            index = index + jnp.where((column & (1 << k)) != 0, source[k], 0)
        goal = jnp.zeros((1, rows), jnp.int32)
        for k in range(upper):
            goal = goal + jnp.where((index & target[k]) != 0, 1 << k, 0)
        perms[slot] = (row == goal).astype(jnp.float32).astype(jnp.bfloat16)

    def make_matrix(number):
        gate_copies[number].wait()
        whole = jnp.concatenate([gates_v[number, 0], gates_v[number, 1]], axis=1)
        high = whole.astype(jnp.bfloat16)
        low = (whole - high.astype(jnp.float32)).astype(jnp.bfloat16)
        mats[number, :gate_dim] = high
        mats[number, gate_dim:] = low

    sign = jnp.where(lax.broadcasted_iota(jnp.int32, (1, LANES), 1) < half, -1.0, 1.0)

    def permuted(values, slot):
        high = values.astype(jnp.bfloat16)
        low = (values - high.astype(jnp.float32)).astype(jnp.bfloat16)
        both = jnp.concatenate([high, low], axis=1)
        moved = jnp.dot(perms[slot], both, preferred_element_type=jnp.float32)
        return moved[:, :LANES], moved[:, LANES:]

    def gate(values, slot, number):
        both = jnp.concatenate(permuted(values, slot), axis=1)
        blocks = []
        for k in range(rest):
            part = both[k * gate_dim : (k + 1) * gate_dim]
            turned = jnp.concatenate(
                [
                    pltpu.roll(part[:, :LANES], half, 1) * sign,
                    pltpu.roll(part[:, LANES:], half, 1) * sign,
                ],
                axis=1,
            )
            whole = jnp.concatenate([part, turned], axis=0).astype(jnp.bfloat16)
            mixed = jnp.dot(mats[number], whole, preferred_element_type=jnp.float32)
            blocks.append(
                mixed[:gate_dim, :LANES]
                + (mixed[gate_dim:, :LANES] + mixed[:gate_dim, LANES:])
            )
        return jnp.concatenate(blocks, axis=0)

    def moved(values, slot):
        high, low = permuted(values, slot)
        return high + low

    def wide_copy(chunk, apart):
        other = lax.rem(wide_me + apart, n_wide)
        return pltpu.make_async_remote_copy(
            src_ref=wide_out.at[chunk, other],
            dst_ref=wide_in.at[chunk, wide_me],
            send_sem=wide_send.at[chunk, apart - 1],
            recv_sem=wide_recv.at[chunk, apart - 1],
            device_id=(other, narrow_me),
            device_id_type=MESH,
        )

    def narrow_copy(chunk, apart):
        other = lax.rem(narrow_me + apart, n_narrow)
        return pltpu.make_async_remote_copy(
            src_ref=narrow_out.at[chunk, other],
            dst_ref=narrow_in.at[chunk, narrow_me],
            send_sem=narrow_send.at[chunk, apart - 1],
            recv_sem=narrow_recv.at[chunk, apart - 1],
            device_id=(wide_me, other),
            device_id_type=MESH,
        )

    slot = 0
    plan = []
    for numbers, leave in zip(stages, (wide_layout, narrow_layout, natural)):
        plan.append((slot, numbers, leave))
        slot += len(numbers) + 1

    def prepare(stage, layout):
        start, numbers, leave = plan[stage]
        for k, number in enumerate(numbers):
            target = gate_layout(number)
            make_perm(start + k, layout, target)
            make_matrix(number)
            layout = target
        make_perm(start + len(numbers), layout, leave)

    def run(values, stage):
        start, numbers, _ = plan[stage]
        for k, number in enumerate(numbers):
            values = gate(values, start + k, number)
        return moved(values, start + len(numbers))

    prepare(0, natural)
    state_copy.wait()
    real = state_v[pl.ds(0, rows, stride=2), :]
    imag = state_v[pl.ds(1, rows, stride=2), :]
    first_half = lax.broadcasted_iota(jnp.int32, (1, LANES), 1) < half
    pieces = (
        jnp.where(first_half, real, pltpu.roll(imag, half, 1)),
        jnp.where(first_half, pltpu.roll(real, half, 1), imag),
    )
    for chunk in range(CHUNKS):
        values = run(pieces[chunk], 0)
        wide_out[chunk] = values.reshape(n_wide, rows // n_wide, LANES)
        if chunk == 0:
            pl.semaphore_wait(barrier, devices - 1)
        for apart in range(1, n_wide):
            wide_copy(chunk, apart).start()
        wide_in[chunk, wide_me] = wide_out[chunk, wide_me]

    prepare(1, wide_layout)
    prepare(2, narrow_layout)
    for chunk in range(CHUNKS):
        for apart in range(1, n_wide):
            wide_copy(chunk, apart).wait_recv()
        values = run(wide_in[chunk].reshape(rows, LANES), 1)
        narrow_out[chunk] = values.reshape(n_narrow, rows // n_narrow, LANES)
        for apart in range(1, n_narrow):
            narrow_copy(chunk, apart).start()
        narrow_in[chunk, narrow_me] = narrow_out[chunk, narrow_me]

    results = []
    for chunk in range(CHUNKS):
        for apart in range(1, n_narrow):
            narrow_copy(chunk, apart).wait_recv()
        results.append(run(narrow_in[chunk].reshape(rows, LANES), 2))

    high = jnp.maximum(results[0], results[1]).max(axis=0, keepdims=True)
    low = -jnp.minimum(results[0], results[1]).min(axis=0, keepdims=True)
    high = jnp.maximum(high, pltpu.roll(high, half, 1))
    low = jnp.maximum(low, pltpu.roll(low, half, 1))
    ext_out[...] = jnp.where(first_half, high, low)

    def ext_copy(apart):
        return pltpu.make_async_remote_copy(
            src_ref=ext_out,
            dst_ref=ext_in.at[apart - 1],
            send_sem=ext_send.at[apart - 1],
            recv_sem=ext_recv.at[apart - 1],
            device_id=device_at(apart),
            device_id_type=MESH,
        )

    for_others(lambda apart: ext_copy(apart).start())
    state_v[:rows] = jnp.where(first_half, results[0], pltpu.roll(results[1], half, 1))
    state_v[rows:] = jnp.where(first_half, pltpu.roll(results[0], half, 1), results[1])
    for chunk in range(CHUNKS):
        for apart in range(1, n_wide):
            wide_copy(chunk, apart).wait_send()
        for apart in range(1, n_narrow):
            narrow_copy(chunk, apart).wait_send()
    for_others(lambda apart: ext_copy(apart).wait_recv())
    total = jnp.maximum(ext_out[...], ext_in[...].max(axis=0))
    highest = jnp.max(jnp.where(first_half, total, -jnp.inf), axis=1, keepdims=True)
    lowest = -jnp.max(jnp.where(first_half, -jnp.inf, total), axis=1, keepdims=True)
    middle = (highest + lowest) * 0.5
    halfwidth = (highest - lowest) * 0.5 + 1e-06
    scale = companding / halfwidth
    for plane in range(2):
        values = (state_v[plane * rows : (plane + 1) * rows] - middle) * scale
        magnitude = jnp.abs(values)
        squared = magnitude * magnitude + 1.0
        grown = jnp.log(magnitude + squared * lax.rsqrt(squared)) * (1.0 / companding_norm)
        out_ref[pl.ds(plane, rows, stride=2), :] = jnp.where(values < 0, -grown, grown)
    for_others(lambda apart: ext_copy(apart).wait_send())


def plain_local(state, gates, gate_qubits, swap_order):
    n_wide = lax.axis_size("wide")
    n_narrow = lax.axis_size("narrow")
    upper = state.shape[1].bit_length() - 1 - LANE_QUBITS
    rows = 2**upper
    gate_count, gate_bits = gate_qubits.shape
    gate_dim = 2**gate_bits
    stages = (range(3), range(3, 6), range(6, gate_count))
    dma = pltpu.SemaphoreType.DMA
    woven = state.reshape(2, rows, LANES).transpose(1, 0, 2).reshape(2 * rows, LANES)
    final = pl.pallas_call(
        functools.partial(plain_kernel, n_wide, n_narrow, upper, gate_bits, stages),
        out_shape=jax.ShapeDtypeStruct((2 * rows, LANES), jnp.float32),
        in_specs=[pl.BlockSpec(memory_space=pltpu.HBM)] * 4,
        out_specs=pl.BlockSpec(memory_space=pltpu.VMEM),
        scratch_shapes=[
            pltpu.SMEM(gate_qubits.shape, jnp.int32),
            pltpu.SMEM(swap_order.shape, jnp.int32),
            pltpu.VMEM((2 * rows, LANES), jnp.float32),
            pltpu.VMEM(gates.shape, jnp.float32),
            pltpu.VMEM((gate_count + 3, rows, rows), jnp.bfloat16),
            pltpu.VMEM((gate_count, 2 * gate_dim, 2 * gate_dim), jnp.bfloat16),
            pltpu.VMEM((CHUNKS, n_wide, rows // n_wide, LANES), jnp.float32),
            pltpu.VMEM((CHUNKS, n_wide, rows // n_wide, LANES), jnp.float32),
            pltpu.VMEM((CHUNKS, n_narrow, rows // n_narrow, LANES), jnp.float32),
            pltpu.VMEM((CHUNKS, n_narrow, rows // n_narrow, LANES), jnp.float32),
            pltpu.VMEM((1, LANES), jnp.float32),
            pltpu.VMEM((n_wide * n_narrow - 1, 1, LANES), jnp.float32),
            dma((3,)),
            dma((gate_count,)),
            dma((CHUNKS, n_wide - 1)),
            dma((CHUNKS, n_wide - 1)),
            dma((CHUNKS, n_narrow - 1)),
            dma((CHUNKS, n_narrow - 1)),
            dma((n_wide * n_narrow - 1,)),
            dma((n_wide * n_narrow - 1,)),
        ],
        compiler_params=pltpu.CompilerParams(
            collective_id=0, has_side_effects=True, vmem_limit_bytes=67043328
        ),
        name="plain_gate_layers",
    )(gate_qubits, swap_order, woven, gates)
    return final.reshape(rows, 2, LANES).transpose(1, 0, 2).reshape(state.shape)


CUTS = (64, 64)


def kernel(
    n_wide,
    n_narrow,
    upper,
    gate_bits,
    stages,
    sizes,
    qubits_hbm,
    swap_hbm,
    state_ref,
    gates_ref,
    out_ref,
    middle_ref,
    scale_ref,
    qubits_ref,
    swap_ref,
    state_v,
    gates_v,
    perms,
    mats,
    turned,
    wide_out,
    wide_in,
    narrow_out,
    narrow_in,
    final,
    ext_out,
    ext_in,
    local_sem,
    gate_sem,
    wide_send,
    wide_recv,
    narrow_send,
    narrow_recv,
    ext_send,
    ext_recv,
    wide_ready,
    narrow_ready,
):
    rows = 2**upper
    gate_dim = 2**gate_bits
    rest = rows // gate_dim
    tiles = rows // LANES
    narrow_bits = n_narrow.bit_length() - 1
    wide_me = lax.axis_index("wide")
    narrow_me = lax.axis_index("narrow")
    half = LANES // 2
    chunks = range(len(sizes))
    starts = [sum(sizes[:k]) for k in chunks]
    devices = n_wide * n_narrow
    f32, bf16 = jnp.float32, jnp.bfloat16

    qubits_copy = pltpu.make_async_copy(qubits_hbm, qubits_ref, local_sem.at[1])
    qubits_copy.start()
    swap_copy = pltpu.make_async_copy(swap_hbm, swap_ref, local_sem.at[2])
    swap_copy.start()
    state_copy = pltpu.make_async_copy(state_ref, state_v, local_sem.at[0])
    state_copy.start()
    gate_copies = []
    for number in range(gates_v.shape[0]):
        copy = pltpu.make_async_copy(
            gates_ref.at[number], gates_v.at[number], gate_sem.at[number]
        )
        copy.start()
        gate_copies.append(copy)

    barrier = pltpu.get_barrier_semaphore()

    def partners(me, count):
        found = [me]
        for k in range(count.bit_length() - 1):
            step = (1 << k) * (1 - 2 * lax.rem(lax.div(me, 1 << k), 2))
            found = found + [other + step for other in found]
        return found

    wide_at = partners(wide_me, n_wide)
    narrow_at = partners(narrow_me, n_narrow)
    others = range(1, devices)

    def device_at(apart):
        return (wide_at[apart // n_narrow], narrow_at[apart % n_narrow])

    def greet_wide(other, _):
        pl.semaphore_signal(
            barrier, inc=1, device_id=(other, narrow_me), device_id_type=MESH
        )

    def greet_narrow(other, _):
        pl.semaphore_signal(barrier, inc=1, device_id=(wide_me, other), device_id_type=MESH)

    lax.fori_loop(wide_me + 1, n_wide, greet_wide, None)
    lax.fori_loop(narrow_me + 1, n_narrow, greet_narrow, None)

    def answer_wide(other, _):
        pl.semaphore_signal(
            wide_ready.at[wide_me], inc=1, device_id=(other, narrow_me), device_id_type=MESH
        )
        pl.semaphore_signal(wide_ready.at[other], inc=1)

    def answer_narrow(other, _):
        pl.semaphore_signal(
            narrow_ready.at[narrow_me], inc=1, device_id=(wide_me, other), device_id_type=MESH
        )
        pl.semaphore_signal(narrow_ready.at[other], inc=1)


    @pl.when(wide_me + narrow_me > 0)
    def _():
        pl.semaphore_wait(barrier, wide_me + narrow_me)

    lax.fori_loop(0, wide_me, answer_wide, None)
    lax.fori_loop(0, narrow_me, answer_narrow, None)

    def gate_layout(number):
        masks = [jnp.int32(1) << (qubits_ref[number, k] - LANE_QUBITS) for k in range(gate_bits)]
        left = jnp.int32(rows - 1)
        for mask in masks:
            left = left - mask
        for _ in range(upper - gate_bits):
            low = left & (-left)
            masks.append(low)
            left = left - low
        return masks

    def swap_layout(order):
        return [jnp.int32(1) << (swap_ref[k] - LANE_QUBITS) for k in order]

    natural = [jnp.int32(1 << k) for k in range(upper)]
    column = lax.broadcasted_iota(jnp.int32, (1, rows), 1)
    row = lax.broadcasted_iota(jnp.int32, (rows, rows), 0)
    first_half = lax.broadcasted_iota(jnp.int32, (1, LANES), 1) < half

    def make_perm(slot, source, target):
        index = jnp.zeros((1, rows), jnp.int32)
        for k in range(upper):
            index = index + jnp.where((column & (1 << k)) != 0, target[k], 0)
        place = jnp.zeros((1, rows), jnp.int32)
        for k in range(upper):
            place = place + jnp.where((index & source[k]) != 0, 1 << k, 0)
        perms[slot] = (row == place).astype(f32).astype(bf16)

    def split(values):
        high = values.astype(bf16)
        return high, (values - high.astype(f32)).astype(bf16)

    def make_matrix(number):
        real = split(gates_v[number, 0].T)
        imag = split(gates_v[number, 1].T)
        for k in range(2):
            top, bottom = 2 * k * gate_dim, (2 * k + 1) * gate_dim
            mats[number, top:bottom, :gate_dim] = real[k]
            mats[number, top:bottom, gate_dim:] = imag[k]
            mats[number, bottom : bottom + gate_dim, :gate_dim] = -imag[k]
            mats[number, bottom : bottom + gate_dim, gate_dim:] = real[k]

    def moved(parts, slot):
        middle = rows // 2
        return jnp.concatenate(
            [
                jnp.dot(parts, perms[slot, :, :middle], preferred_element_type=f32),
                jnp.dot(parts, perms[slot, :, middle:], preferred_element_type=f32),
            ],
            axis=1,
        )

    def gate(parts, slot, number):
        count = parts.shape[0] // 4
        parts = moved(parts, slot).astype(bf16)

        def side(first):
            return jnp.concatenate(
                [
                    jnp.concatenate(
                        [
                            parts[first : first + count, k * gate_dim : (k + 1) * gate_dim],
                            parts[first + count : first + 2 * count, k * gate_dim : (k + 1) * gate_dim],
                        ],
                        axis=1,
                    )
                    for k in range(rest)
                ],
                axis=0,
            )

        high, low = side(0), side(2 * count)
        weights = jnp.concatenate([mats[number, : 2 * gate_dim], mats[number]], axis=0)
        whole = jnp.concatenate([high, low, high], axis=1)
        middle = whole.shape[0] // 2
        mixed = jnp.concatenate(
            [
                jnp.dot(whole[:middle], weights, preferred_element_type=f32),
                jnp.dot(whole[middle:], weights, preferred_element_type=f32),
            ],
            axis=0,
        )
        return jnp.concatenate(
            [
                jnp.concatenate(
                    [
                        part[k * count : (k + 1) * count, plane * gate_dim : (plane + 1) * gate_dim]
                        for k in range(rest)
                    ],
                    axis=1,
                )
                for part in split(mixed)
                for plane in range(2)
            ],
            axis=0,
        )

    slot = 0
    plan = []
    for numbers in stages:
        plan.append((slot, numbers))
        slot += len(numbers) + 1

    def prepare(stage, layout, leave):
        start, numbers = plan[stage]
        for k, number in enumerate(numbers):
            target = gate_layout(number)
            make_perm(start + k, layout, target)
            make_matrix(number)
            layout = target
        make_perm(start + len(numbers), layout, leave)

    def run(parts, stage):
        start, numbers = plan[stage]
        for k, number in enumerate(numbers):
            parts = gate(parts, start + k, number)
        both = moved(parts, start + len(numbers))
        count = both.shape[0] // 2
        return both[:count] + both[count:]

    def wide_copy(chunk, apart):
        other = wide_at[apart]
        part = pl.ds(starts[chunk], sizes[chunk])
        return pltpu.make_async_remote_copy(
            src_ref=wide_out.at[other, part],
            dst_ref=wide_in.at[wide_me, part],
            send_sem=wide_send.at[chunk, apart - 1],
            recv_sem=wide_recv.at[chunk, apart - 1],
            device_id=(other, narrow_me),
            device_id_type=MESH,
        )

    def narrow_copy(chunk, apart):
        other = narrow_at[apart]
        part = pl.ds(2 * starts[chunk], 2 * sizes[chunk])
        return pltpu.make_async_remote_copy(
            src_ref=narrow_out.at[other, part],
            dst_ref=narrow_in.at[narrow_me, part],
            send_sem=narrow_send.at[chunk, apart - 1],
            recv_sem=narrow_recv.at[chunk, apart - 1],
            device_id=(wide_me, other),
            device_id_type=MESH,
        )

    def ext_copy(apart):
        return pltpu.make_async_remote_copy(
            src_ref=ext_out,
            dst_ref=ext_in.at[apart - 1],
            send_sem=ext_send.at[apart - 1],
            recv_sem=ext_recv.at[apart - 1],
            device_id=device_at(apart),
            device_id_type=MESH,
        )

    def first_stage(chunk):
        first, count = starts[chunk], sizes[chunk]
        parts = jnp.concatenate(
            [turned[k, first : first + count] for k in range(4)], axis=0
        )
        both = run(parts, 0)
        real, imag = both[:count], both[count:]
        for m in range(tiles):
            re, im = real[:, m * LANES : (m + 1) * LANES], imag[:, m * LANES : (m + 1) * LANES]
            wide_out[2 * m, first : first + count] = jnp.where(
                first_half, re, pltpu.roll(im, half, 1)
            )
            wide_out[2 * m + 1, first : first + count] = jnp.where(
                first_half, pltpu.roll(re, half, 1), im
            )

    def first_send(chunk):
        for apart in range(1, n_wide):
            if chunk == 0:
                pl.semaphore_wait(wide_ready.at[wide_at[apart]], 1)
            wide_copy(chunk, apart).start()
        part = pl.ds(starts[chunk], sizes[chunk])
        wide_in[wide_me, part] = wide_out[wide_me, part]

    def second_stage(chunk):
        first, count = starts[chunk], sizes[chunk]
        for apart in range(1, n_wide):
            wide_copy(chunk, apart).wait_recv()
        real, imag = [], []
        for m in range(tiles):
            left = wide_in[2 * m, first : first + count]
            right = wide_in[2 * m + 1, first : first + count]
            real.append(jnp.where(first_half, left, pltpu.roll(right, half, 1)))
            imag.append(jnp.where(first_half, pltpu.roll(left, half, 1), right))
        whole = jnp.concatenate(
            [jnp.concatenate(real, axis=1), jnp.concatenate(imag, axis=1)], axis=0
        )
        both = run(jnp.concatenate(split(whole), axis=0), 1)
        width = rows // n_narrow
        for m in range(n_narrow):
            narrow_out[m, 2 * first : 2 * (first + count)] = both[:, m * width : (m + 1) * width]

    def second_send(chunk):
        for apart in range(1, n_narrow):
            if chunk == 0:
                pl.semaphore_wait(narrow_ready.at[narrow_at[apart]], 1)
            narrow_copy(chunk, apart).start()
        part = pl.ds(2 * starts[chunk], 2 * sizes[chunk])
        narrow_in[narrow_me, part] = narrow_out[narrow_me, part]

    def third_stage(chunk):
        first, count = starts[chunk], sizes[chunk]
        for apart in range(1, n_narrow):
            narrow_copy(chunk, apart).wait_recv()
        whole = jnp.concatenate(
            [narrow_in[m, 2 * first : 2 * (first + count)] for m in range(n_narrow)], axis=1
        )
        both = run(jnp.concatenate(split(whole), axis=0), 2)
        final[0, first : first + count] = both[:count]
        final[1, first : first + count] = both[count:]

    qubits_copy.wait()
    swap_copy.wait()
    state_copy.wait()
    for number in stages[0]:
        gate_copies[number].wait()
    wide_layout = swap_layout(range(upper))
    narrow_layout = swap_layout(list(range(narrow_bits, upper)) + list(range(narrow_bits)))
    prepare(0, natural, wide_layout)
    for plane in range(2):
        high, low = split(state_v[pl.ds(plane, rows, stride=2), :].T)
        turned[plane] = high
        turned[2 + plane] = low
    for chunk in chunks:
        first_stage(chunk)
        first_send(chunk)

    for number in range(stages[1][0], gates_v.shape[0]):
        gate_copies[number].wait()
    prepare(1, wide_layout, narrow_layout)
    prepare(2, narrow_layout, natural)

    last = len(sizes) - 1
    for chunk in chunks:
        second_stage(chunk)
        second_send(chunk)
        if chunk > 0:
            third_stage(chunk - 1)
    third_stage(last)

    whole = final[...]
    high, low = whole.max(axis=0), -whole.min(axis=0)
    for k, value in enumerate((high, low)):
        value = value.max(axis=0, keepdims=True)
        ext_out[k : k + 1] = functools.reduce(
            jnp.maximum, [value[:, m * LANES : (m + 1) * LANES] for m in range(tiles)]
        )
    for apart in others:
        ext_copy(apart).start()

    for plane in range(2):
        out_ref[pl.ds(plane, rows, stride=2), :] = final[plane].T
    for chunk in chunks:
        for apart in range(1, n_wide):
            wide_copy(chunk, apart).wait_send()
        for apart in range(1, n_narrow):
            narrow_copy(chunk, apart).wait_send()

    for apart in others:
        ext_copy(apart).wait_recv()
    total = jnp.maximum(ext_out[...], ext_in[...].max(axis=0))
    total = jnp.max(total, axis=1, keepdims=True)
    highest, lowest = total[0:1], -total[1:2]
    middle = (highest + lowest) * 0.5
    halfwidth = (highest - lowest) * 0.5 + 1e-06
    middle_ref[...] = jnp.broadcast_to(middle, (1, LANES))
    scale_ref[...] = jnp.broadcast_to(companding / halfwidth, (1, LANES))
    for apart in others:
        ext_copy(apart).wait_send()


def local(state, gates, gate_qubits, swap_order):
    n_wide = lax.axis_size("wide")
    n_narrow = lax.axis_size("narrow")
    upper = state.shape[1].bit_length() - 1 - LANE_QUBITS
    rows = 2**upper
    gate_count, gate_bits = gate_qubits.shape
    gate_dim = 2**gate_bits
    devices = n_wide * n_narrow
    if 2 * rows != n_wide * LANES or rows != n_narrow * LANES or gate_dim != LANES:
        return plain_local(state, gates, gate_qubits, swap_order)
    stages = (range(3), range(3, 6), range(6, gate_count))
    dma = pltpu.SemaphoreType.DMA
    bf16, f32 = jnp.bfloat16, jnp.float32
    sizes = [cut * LANES // sum(CUTS) for cut in CUTS]
    chunks = len(sizes)
    woven = state.reshape(2, rows, LANES).transpose(1, 0, 2).reshape(2 * rows, LANES)
    held = [
        pltpu.with_memory_space_constraint(x, pltpu.HBM)
        for x in (gate_qubits, swap_order, woven, gates)
    ]
    final, middle, scale = pl.pallas_call(
        functools.partial(kernel, n_wide, n_narrow, upper, gate_bits, stages, sizes),
        out_shape=(
            pltpu.VMEM((2 * rows, LANES), f32),
            pltpu.VMEM((1, LANES), f32),
            pltpu.VMEM((1, LANES), f32),
        ),
        in_specs=[pl.BlockSpec(memory_space=pltpu.HBM)] * 4,
        out_specs=[pl.BlockSpec(memory_space=pltpu.VMEM)] * 3,
        scratch_shapes=[
            pltpu.SMEM(gate_qubits.shape, jnp.int32),
            pltpu.SMEM(swap_order.shape, jnp.int32),
            pltpu.VMEM((2 * rows, LANES), f32),
            pltpu.VMEM(gates.shape, f32),
            pltpu.VMEM((gate_count + 3, rows, rows), bf16),
            pltpu.VMEM((gate_count, 4 * gate_dim, 2 * gate_dim), bf16),
            pltpu.VMEM((4, LANES, rows), bf16),
            pltpu.VMEM((n_wide, LANES, LANES), f32),
            pltpu.VMEM((n_wide, LANES, LANES), f32),
            pltpu.VMEM((n_narrow, 2 * LANES, LANES), f32),
            pltpu.VMEM((n_narrow, 2 * LANES, LANES), f32),
            pltpu.VMEM((2, LANES, rows), f32),
            pltpu.VMEM((2, LANES), f32),
            pltpu.VMEM((devices - 1, 2, LANES), f32),
            dma((3,)),
            dma((gate_count,)),
            dma((chunks, n_wide - 1)),
            dma((chunks, n_wide - 1)),
            dma((chunks, n_narrow - 1)),
            dma((chunks, n_narrow - 1)),
            dma((devices - 1,)),
            dma((devices - 1,)),
            pltpu.SemaphoreType.REGULAR((n_wide,)),
            pltpu.SemaphoreType.REGULAR((n_narrow,)),
        ],
        compiler_params=pltpu.CompilerParams(
            collective_id=0, has_side_effects=True, vmem_limit_bytes=40000000
        ),
        name="gate_layers",
    )(*held)
    values = (final - middle) * scale
    magnitude = jnp.abs(values)
    squared = magnitude * magnitude + 1.0
    grown = jnp.log(magnitude + squared * lax.rsqrt(squared)) * (1.0 / companding_norm)
    final = jnp.where(values < 0, -grown, grown)
    return final.reshape(rows, 2, LANES).transpose(1, 0, 2).reshape(state.shape)


def solution(mesh):
    in_specs = (P(None, ("wide", "narrow")), P(), P(), P())
    out_specs = P(None, ("wide", "narrow"))
    return jax.shard_map(local, mesh=mesh, in_specs=in_specs, out_specs=out_specs, check_vma=False)
```

```python
import functools
import math

import jax
import jax.numpy as jnp
from jax import lax
from jax.experimental import pallas as pl
from jax.experimental.pallas import tpu as pltpu
from jax.sharding import PartitionSpec as P

LANE_QUBITS = 7
LANES = 2**LANE_QUBITS
CHUNKS = 2

companding = 16.0
companding_norm = math.log(16.0 + math.sqrt(257.0))

MESH = pl.DeviceIdType.MESH


def plain_kernel(
    n_wide,
    n_narrow,
    upper,
    gate_bits,
    stages,
    qubits_hbm,
    swap_hbm,
    state_ref,
    gates_ref,
    out_ref,
    qubits_ref,
    swap_ref,
    state_v,
    gates_v,
    perms,
    mats,
    wide_out,
    wide_in,
    narrow_out,
    narrow_in,
    ext_out,
    ext_in,
    local_sem,
    gate_sem,
    wide_send,
    wide_recv,
    narrow_send,
    narrow_recv,
    ext_send,
    ext_recv,
):
    rows = 2**upper
    gate_dim = 2**gate_bits
    rest = rows // gate_dim
    wide_bits = n_wide.bit_length() - 1
    narrow_bits = n_narrow.bit_length() - 1
    wide_me = lax.axis_index("wide")
    narrow_me = lax.axis_index("narrow")
    half = LANES // 2

    qubits_copy = pltpu.make_async_copy(qubits_hbm, qubits_ref, local_sem.at[1])
    qubits_copy.start()
    swap_copy = pltpu.make_async_copy(swap_hbm, swap_ref, local_sem.at[2])
    swap_copy.start()
    state_copy = pltpu.make_async_copy(state_ref, state_v, local_sem.at[0])
    state_copy.start()
    gate_copies = []
    for number in range(gates_v.shape[0]):
        copy = pltpu.make_async_copy(
            gates_ref.at[number], gates_v.at[number], gate_sem.at[number]
        )
        copy.start()
        gate_copies.append(copy)

    barrier = pltpu.get_barrier_semaphore()
    devices = n_wide * n_narrow
    flat_me = wide_me * n_narrow + narrow_me

    def device_at(apart):
        other = lax.rem(flat_me + apart, devices)
        return (lax.div(other, n_narrow), lax.rem(other, n_narrow))

    def for_others(step):
        if devices <= 64:
            for apart in range(1, devices):
                step(apart)
        else:
            lax.fori_loop(1, devices, lambda apart, _: step(apart), None)

    def greet(apart):
        pl.semaphore_signal(barrier, inc=1, device_id=device_at(apart), device_id_type=MESH)

    for_others(greet)
    qubits_copy.wait()
    swap_copy.wait()

    def gate_layout(number):
        masks = [jnp.int32(1) << (qubits_ref[number, k] - LANE_QUBITS) for k in range(gate_bits)]
        left = jnp.int32(rows - 1)
        for mask in masks:
            left = left - mask
        for _ in range(upper - gate_bits):
            low = left & (-left)
            masks.append(low)
            left = left - low
        return masks

    def swap_layout(order):
        return [jnp.int32(1) << (swap_ref[k] - LANE_QUBITS) for k in order]

    natural = [jnp.int32(1 << k) for k in range(upper)]
    wide_layout = swap_layout(range(upper))
    narrow_layout = swap_layout(list(range(narrow_bits, upper)) + list(range(narrow_bits)))

    column = lax.broadcasted_iota(jnp.int32, (1, rows), 1)
    row = lax.broadcasted_iota(jnp.int32, (rows, rows), 0)

    def make_perm(slot, source, target):
        index = jnp.zeros((1, rows), jnp.int32)
        for k in range(upper):
            index = index + jnp.where((column & (1 << k)) != 0, source[k], 0)
        goal = jnp.zeros((1, rows), jnp.int32)
        for k in range(upper):
            goal = goal + jnp.where((index & target[k]) != 0, 1 << k, 0)
        perms[slot] = (row == goal).astype(jnp.float32).astype(jnp.bfloat16)

    def make_matrix(number):
        gate_copies[number].wait()
        whole = jnp.concatenate([gates_v[number, 0], gates_v[number, 1]], axis=1)
        high = whole.astype(jnp.bfloat16)
        low = (whole - high.astype(jnp.float32)).astype(jnp.bfloat16)
        mats[number, :gate_dim] = high
        mats[number, gate_dim:] = low

    sign = jnp.where(lax.broadcasted_iota(jnp.int32, (1, LANES), 1) < half, -1.0, 1.0)

    def permuted(values, slot):
        high = values.astype(jnp.bfloat16)
        low = (values - high.astype(jnp.float32)).astype(jnp.bfloat16)
        both = jnp.concatenate([high, low], axis=1)
        moved = jnp.dot(perms[slot], both, preferred_element_type=jnp.float32)
        return moved[:, :LANES], moved[:, LANES:]

    def gate(values, slot, number):
        both = jnp.concatenate(permuted(values, slot), axis=1)
        blocks = []
        for k in range(rest):
            part = both[k * gate_dim : (k + 1) * gate_dim]
            turned = jnp.concatenate(
                [
                    pltpu.roll(part[:, :LANES], half, 1) * sign,
                    pltpu.roll(part[:, LANES:], half, 1) * sign,
                ],
                axis=1,
            )
            whole = jnp.concatenate([part, turned], axis=0).astype(jnp.bfloat16)
            mixed = jnp.dot(mats[number], whole, preferred_element_type=jnp.float32)
            blocks.append(
                mixed[:gate_dim, :LANES]
                + (mixed[gate_dim:, :LANES] + mixed[:gate_dim, LANES:])
            )
        return jnp.concatenate(blocks, axis=0)

    def moved(values, slot):
        high, low = permuted(values, slot)
        return high + low

    def wide_copy(chunk, apart):
        other = lax.rem(wide_me + apart, n_wide)
        return pltpu.make_async_remote_copy(
            src_ref=wide_out.at[chunk, other],
            dst_ref=wide_in.at[chunk, wide_me],
            send_sem=wide_send.at[chunk, apart - 1],
            recv_sem=wide_recv.at[chunk, apart - 1],
            device_id=(other, narrow_me),
            device_id_type=MESH,
        )

    def narrow_copy(chunk, apart):
        other = lax.rem(narrow_me + apart, n_narrow)
        return pltpu.make_async_remote_copy(
            src_ref=narrow_out.at[chunk, other],
            dst_ref=narrow_in.at[chunk, narrow_me],
            send_sem=narrow_send.at[chunk, apart - 1],
            recv_sem=narrow_recv.at[chunk, apart - 1],
            device_id=(wide_me, other),
            device_id_type=MESH,
        )

    slot = 0
    plan = []
    for numbers, leave in zip(stages, (wide_layout, narrow_layout, natural)):
        plan.append((slot, numbers, leave))
        slot += len(numbers) + 1

    def prepare(stage, layout):
        start, numbers, leave = plan[stage]
        for k, number in enumerate(numbers):
            target = gate_layout(number)
            make_perm(start + k, layout, target)
            make_matrix(number)
            layout = target
        make_perm(start + len(numbers), layout, leave)

    def run(values, stage):
        start, numbers, _ = plan[stage]
        for k, number in enumerate(numbers):
            values = gate(values, start + k, number)
        return moved(values, start + len(numbers))

    prepare(0, natural)
    state_copy.wait()
    real = state_v[pl.ds(0, rows, stride=2), :]
    imag = state_v[pl.ds(1, rows, stride=2), :]
    first_half = lax.broadcasted_iota(jnp.int32, (1, LANES), 1) < half
    pieces = (
        jnp.where(first_half, real, pltpu.roll(imag, half, 1)),
        jnp.where(first_half, pltpu.roll(real, half, 1), imag),
    )
    for chunk in range(CHUNKS):
        values = run(pieces[chunk], 0)
        wide_out[chunk] = values.reshape(n_wide, rows // n_wide, LANES)
        if chunk == 0:
            pl.semaphore_wait(barrier, devices - 1)
        for apart in range(1, n_wide):
            wide_copy(chunk, apart).start()
        wide_in[chunk, wide_me] = wide_out[chunk, wide_me]

    prepare(1, wide_layout)
    prepare(2, narrow_layout)
    for chunk in range(CHUNKS):
        for apart in range(1, n_wide):
            wide_copy(chunk, apart).wait_recv()
        values = run(wide_in[chunk].reshape(rows, LANES), 1)
        narrow_out[chunk] = values.reshape(n_narrow, rows // n_narrow, LANES)
        for apart in range(1, n_narrow):
            narrow_copy(chunk, apart).start()
        narrow_in[chunk, narrow_me] = narrow_out[chunk, narrow_me]

    results = []
    for chunk in range(CHUNKS):
        for apart in range(1, n_narrow):
            narrow_copy(chunk, apart).wait_recv()
        results.append(run(narrow_in[chunk].reshape(rows, LANES), 2))

    high = jnp.maximum(results[0], results[1]).max(axis=0, keepdims=True)
    low = -jnp.minimum(results[0], results[1]).min(axis=0, keepdims=True)
    high = jnp.maximum(high, pltpu.roll(high, half, 1))
    low = jnp.maximum(low, pltpu.roll(low, half, 1))
    ext_out[...] = jnp.where(first_half, high, low)

    def ext_copy(apart):
        return pltpu.make_async_remote_copy(
            src_ref=ext_out,
            dst_ref=ext_in.at[apart - 1],
            send_sem=ext_send.at[apart - 1],
            recv_sem=ext_recv.at[apart - 1],
            device_id=device_at(apart),
            device_id_type=MESH,
        )

    for_others(lambda apart: ext_copy(apart).start())
    state_v[:rows] = jnp.where(first_half, results[0], pltpu.roll(results[1], half, 1))
    state_v[rows:] = jnp.where(first_half, pltpu.roll(results[0], half, 1), results[1])
    for chunk in range(CHUNKS):
        for apart in range(1, n_wide):
            wide_copy(chunk, apart).wait_send()
        for apart in range(1, n_narrow):
            narrow_copy(chunk, apart).wait_send()
    for_others(lambda apart: ext_copy(apart).wait_recv())
    total = jnp.maximum(ext_out[...], ext_in[...].max(axis=0))
    highest = jnp.max(jnp.where(first_half, total, -jnp.inf), axis=1, keepdims=True)
    lowest = -jnp.max(jnp.where(first_half, -jnp.inf, total), axis=1, keepdims=True)
    middle = (highest + lowest) * 0.5
    halfwidth = (highest - lowest) * 0.5 + 1e-06
    scale = companding / halfwidth
    for plane in range(2):
        values = (state_v[plane * rows : (plane + 1) * rows] - middle) * scale
        magnitude = jnp.abs(values)
        squared = magnitude * magnitude + 1.0
        grown = jnp.log(magnitude + squared * lax.rsqrt(squared)) * (1.0 / companding_norm)
        out_ref[pl.ds(plane, rows, stride=2), :] = jnp.where(values < 0, -grown, grown)
    for_others(lambda apart: ext_copy(apart).wait_send())


def plain_local(state, gates, gate_qubits, swap_order):
    n_wide = lax.axis_size("wide")
    n_narrow = lax.axis_size("narrow")
    upper = state.shape[1].bit_length() - 1 - LANE_QUBITS
    rows = 2**upper
    gate_count, gate_bits = gate_qubits.shape
    gate_dim = 2**gate_bits
    stages = (range(3), range(3, 6), range(6, gate_count))
    dma = pltpu.SemaphoreType.DMA
    woven = state.reshape(2, rows, LANES).transpose(1, 0, 2).reshape(2 * rows, LANES)
    final = pl.pallas_call(
        functools.partial(plain_kernel, n_wide, n_narrow, upper, gate_bits, stages),
        out_shape=jax.ShapeDtypeStruct((2 * rows, LANES), jnp.float32),
        in_specs=[pl.BlockSpec(memory_space=pltpu.HBM)] * 4,
        out_specs=pl.BlockSpec(memory_space=pltpu.VMEM),
        scratch_shapes=[
            pltpu.SMEM(gate_qubits.shape, jnp.int32),
            pltpu.SMEM(swap_order.shape, jnp.int32),
            pltpu.VMEM((2 * rows, LANES), jnp.float32),
            pltpu.VMEM(gates.shape, jnp.float32),
            pltpu.VMEM((gate_count + 3, rows, rows), jnp.bfloat16),
            pltpu.VMEM((gate_count, 2 * gate_dim, 2 * gate_dim), jnp.bfloat16),
            pltpu.VMEM((CHUNKS, n_wide, rows // n_wide, LANES), jnp.float32),
            pltpu.VMEM((CHUNKS, n_wide, rows // n_wide, LANES), jnp.float32),
            pltpu.VMEM((CHUNKS, n_narrow, rows // n_narrow, LANES), jnp.float32),
            pltpu.VMEM((CHUNKS, n_narrow, rows // n_narrow, LANES), jnp.float32),
            pltpu.VMEM((1, LANES), jnp.float32),
            pltpu.VMEM((n_wide * n_narrow - 1, 1, LANES), jnp.float32),
            dma((3,)),
            dma((gate_count,)),
            dma((CHUNKS, n_wide - 1)),
            dma((CHUNKS, n_wide - 1)),
            dma((CHUNKS, n_narrow - 1)),
            dma((CHUNKS, n_narrow - 1)),
            dma((n_wide * n_narrow - 1,)),
            dma((n_wide * n_narrow - 1,)),
        ],
        compiler_params=pltpu.CompilerParams(
            collective_id=0, has_side_effects=True, vmem_limit_bytes=67043328
        ),
        name="plain_gate_layers",
    )(gate_qubits, swap_order, woven, gates)
    return final.reshape(rows, 2, LANES).transpose(1, 0, 2).reshape(state.shape)


CUTS = (64, 64)


def kernel(
    n_wide,
    n_narrow,
    upper,
    gate_bits,
    stages,
    sizes,
    qubits_hbm,
    swap_hbm,
    state_ref,
    gates_ref,
    out_ref,
    middle_ref,
    scale_ref,
    qubits_ref,
    swap_ref,
    state_v,
    gates_v,
    perms,
    mats,
    turned,
    wide_out,
    wide_in,
    narrow_out,
    narrow_in,
    final,
    ext_out,
    ext_in,
    local_sem,
    wide_send,
    wide_recv,
    narrow_send,
    narrow_recv,
    ext_send,
    ext_recv,
    wide_ready,
    narrow_ready,
):
    rows = 2**upper
    gate_dim = 2**gate_bits
    rest = rows // gate_dim
    tiles = rows // LANES
    narrow_bits = n_narrow.bit_length() - 1
    wide_me = lax.axis_index("wide")
    narrow_me = lax.axis_index("narrow")
    half = LANES // 2
    chunks = range(len(sizes))
    starts = [sum(sizes[:k]) for k in chunks]
    devices = n_wide * n_narrow
    f32, bf16 = jnp.float32, jnp.bfloat16

    qubits_copy = pltpu.make_async_copy(qubits_hbm, qubits_ref, local_sem.at[1])
    qubits_copy.start()
    swap_copy = pltpu.make_async_copy(swap_hbm, swap_ref, local_sem.at[2])
    swap_copy.start()
    state_copy = pltpu.make_async_copy(state_ref, state_v, local_sem.at[0])
    state_copy.start()
    soon = len(stages[0])
    gate_copies = [
        pltpu.make_async_copy(
            gates_ref.at[first:after], gates_v.at[first:after], local_sem.at[3 + k]
        )
        for k, (first, after) in enumerate(((0, soon), (soon, gates_v.shape[0])))
    ]
    for copy in gate_copies:
        copy.start()

    barrier = pltpu.get_barrier_semaphore()

    def partners(me, count):
        found = [me]
        for k in range(count.bit_length() - 1):
            step = (1 << k) * (1 - 2 * lax.rem(lax.div(me, 1 << k), 2))
            found = found + [other + step for other in found]
        return found

    wide_at = partners(wide_me, n_wide)
    narrow_at = partners(narrow_me, n_narrow)
    others = range(devices - 1, 0, -1)

    def device_at(apart):
        return (wide_at[apart // n_narrow], narrow_at[apart % n_narrow])

    def greet_wide(other, _):
        pl.semaphore_signal(
            barrier, inc=1, device_id=(other, narrow_me), device_id_type=MESH
        )

    def greet_narrow(other, _):
        pl.semaphore_signal(barrier, inc=1, device_id=(wide_me, other), device_id_type=MESH)

    lax.fori_loop(wide_me + 1, n_wide, greet_wide, None)
    lax.fori_loop(narrow_me + 1, n_narrow, greet_narrow, None)

    def answer_wide(other, _):
        pl.semaphore_signal(
            wide_ready.at[wide_me], inc=1, device_id=(other, narrow_me), device_id_type=MESH
        )
        pl.semaphore_signal(wide_ready.at[other], inc=1)

    def answer_narrow(other, _):
        pl.semaphore_signal(
            narrow_ready.at[narrow_me], inc=1, device_id=(wide_me, other), device_id_type=MESH
        )
        pl.semaphore_signal(narrow_ready.at[other], inc=1)


    @pl.when(wide_me + narrow_me > 0)
    def _():
        pl.semaphore_wait(barrier, wide_me + narrow_me)

    lax.fori_loop(0, wide_me, answer_wide, None)
    lax.fori_loop(0, narrow_me, answer_narrow, None)

    def gate_layout(number):
        masks = [jnp.int32(1) << (qubits_ref[number, k] - LANE_QUBITS) for k in range(gate_bits)]
        left = jnp.int32(rows - 1)
        for mask in masks:
            left = left - mask
        for _ in range(upper - gate_bits):
            low = left & (-left)
            masks.append(low)
            left = left - low
        return masks

    def swap_layout(order):
        return [jnp.int32(1) << (swap_ref[k] - LANE_QUBITS) for k in order]

    natural = [jnp.int32(1 << k) for k in range(upper)]
    column = lax.broadcasted_iota(jnp.int32, (1, rows), 1)
    row = lax.broadcasted_iota(jnp.int32, (rows, rows), 0).astype(jnp.int16)
    first_half = lax.broadcasted_iota(jnp.int32, (1, LANES), 1) < half

    def make_perm(slot, source, target):
        index = jnp.zeros((1, rows), jnp.int32)
        for k in range(upper):
            index = index + jnp.where((column & (1 << k)) != 0, target[k], 0)
        place = jnp.zeros((1, rows), jnp.int32)
        for k in range(upper):
            place = place + jnp.where((index & source[k]) != 0, 1 << k, 0)
        perms[slot] = jnp.where(row == place.astype(jnp.int16), bf16(1), bf16(0))

    def split(values):
        high = values.astype(bf16)
        return high, (values - high.astype(f32)).astype(bf16)

    def make_matrix(number):
        real = split(gates_v[number, 0].T)
        imag = split(gates_v[number, 1].T)
        for k in range(2):
            top, bottom = 2 * k * gate_dim, (2 * k + 1) * gate_dim
            mats[number, top:bottom, :gate_dim] = real[k]
            mats[number, top:bottom, gate_dim:] = imag[k]
            mats[number, bottom : bottom + gate_dim, :gate_dim] = -imag[k]
            mats[number, bottom : bottom + gate_dim, gate_dim:] = real[k]

    def moved(parts, slot):
        middle = rows // 2
        return jnp.concatenate(
            [
                jnp.dot(parts, perms[slot, :, :middle], preferred_element_type=f32),
                jnp.dot(parts, perms[slot, :, middle:], preferred_element_type=f32),
            ],
            axis=1,
        )

    def gate(parts, slot, number):
        count = parts.shape[0] // 4
        parts = moved(parts, slot).astype(bf16)

        def side(first):
            return jnp.concatenate(
                [
                    jnp.concatenate(
                        [
                            parts[first : first + count, k * gate_dim : (k + 1) * gate_dim],
                            parts[first + count : first + 2 * count, k * gate_dim : (k + 1) * gate_dim],
                        ],
                        axis=1,
                    )
                    for k in range(rest)
                ],
                axis=0,
            )

        high, low = side(0), side(2 * count)
        weights = jnp.concatenate([mats[number, : 2 * gate_dim], mats[number]], axis=0)
        whole = jnp.concatenate([high, low, high], axis=1)
        middle = whole.shape[0] // 2
        mixed = jnp.concatenate(
            [
                jnp.dot(whole[:middle], weights, preferred_element_type=f32),
                jnp.dot(whole[middle:], weights, preferred_element_type=f32),
            ],
            axis=0,
        )
        return jnp.concatenate(
            [
                jnp.concatenate(
                    [
                        part[k * count : (k + 1) * count, plane * gate_dim : (plane + 1) * gate_dim]
                        for k in range(rest)
                    ],
                    axis=1,
                )
                for part in split(mixed)
                for plane in range(2)
            ],
            axis=0,
        )

    slot = 0
    plan = []
    for numbers in stages:
        plan.append((slot, numbers))
        slot += len(numbers) + 1

    def prepare(stage, layout, leave):
        start, numbers = plan[stage]
        for k, number in enumerate(numbers):
            target = gate_layout(number)
            make_perm(start + k, layout, target)
            make_matrix(number)
            layout = target
        make_perm(start + len(numbers), layout, leave)

    def run(parts, stage):
        start, numbers = plan[stage]
        for k, number in enumerate(numbers):
            parts = gate(parts, start + k, number)
        both = moved(parts, start + len(numbers))
        count = both.shape[0] // 2
        return both[:count] + both[count:]

    def wide_copy(chunk, apart):
        other = wide_at[apart]
        part = pl.ds(starts[chunk], sizes[chunk])
        return pltpu.make_async_remote_copy(
            src_ref=wide_out.at[other, part],
            dst_ref=wide_in.at[wide_me, part],
            send_sem=wide_send.at[chunk],
            recv_sem=wide_recv.at[chunk],
            device_id=(other, narrow_me),
            device_id_type=MESH,
        )

    def narrow_copy(chunk, apart):
        other = narrow_at[apart]
        part = pl.ds(2 * starts[chunk], 2 * sizes[chunk])
        return pltpu.make_async_remote_copy(
            src_ref=narrow_out.at[other, part],
            dst_ref=narrow_in.at[narrow_me, part],
            send_sem=narrow_send.at[chunk],
            recv_sem=narrow_recv.at[chunk],
            device_id=(wide_me, other),
            device_id_type=MESH,
        )

    def ext_copy(apart):
        return pltpu.make_async_remote_copy(
            src_ref=ext_out,
            dst_ref=ext_in.at[apart - 1],
            send_sem=ext_send.at[0],
            recv_sem=ext_recv.at[0],
            device_id=device_at(apart),
            device_id_type=MESH,
        )

    def await_wide(chunk, sems):
        all_of = wide_in.at[: n_wide - 1, pl.ds(starts[chunk], sizes[chunk])]
        pltpu.make_async_copy(all_of, all_of, sems.at[chunk]).wait()

    def await_narrow(chunk, sems):
        all_of = narrow_in.at[: n_narrow - 1, pl.ds(2 * starts[chunk], 2 * sizes[chunk])]
        pltpu.make_async_copy(all_of, all_of, sems.at[chunk]).wait()

    def await_ext(sems):
        pltpu.make_async_copy(ext_in, ext_in, sems.at[0]).wait()

    def first_stage(chunk):
        first, count = starts[chunk], sizes[chunk]
        parts = jnp.concatenate(
            [turned[k, first : first + count] for k in range(4)], axis=0
        )
        both = run(parts, 0)
        real, imag = both[:count], both[count:]
        for m in range(tiles):
            re, im = real[:, m * LANES : (m + 1) * LANES], imag[:, m * LANES : (m + 1) * LANES]
            wide_out[2 * m, first : first + count] = jnp.where(
                first_half, re, pltpu.roll(im, half, 1)
            )
            wide_out[2 * m + 1, first : first + count] = jnp.where(
                first_half, pltpu.roll(re, half, 1), im
            )

    def first_send(chunk):
        for apart in range(1, n_wide):
            if chunk == 0:
                pl.semaphore_wait(wide_ready.at[wide_at[apart]], 1)
            wide_copy(chunk, apart).start()
        part = pl.ds(starts[chunk], sizes[chunk])
        wide_in[wide_me, part] = wide_out[wide_me, part]

    def second_stage(chunk):
        first, count = starts[chunk], sizes[chunk]
        await_wide(chunk, wide_recv)
        real, imag = [], []
        for m in range(tiles):
            left = wide_in[2 * m, first : first + count]
            right = wide_in[2 * m + 1, first : first + count]
            real.append(jnp.where(first_half, left, pltpu.roll(right, half, 1)))
            imag.append(jnp.where(first_half, pltpu.roll(left, half, 1), right))
        whole = jnp.concatenate(
            [jnp.concatenate(real, axis=1), jnp.concatenate(imag, axis=1)], axis=0
        )
        both = run(jnp.concatenate(split(whole), axis=0), 1)
        width = rows // n_narrow
        for m in range(n_narrow):
            narrow_out[m, 2 * first : 2 * (first + count)] = both[:, m * width : (m + 1) * width]

    def second_send(chunk):
        for apart in range(1, n_narrow):
            if chunk == 0:
                pl.semaphore_wait(narrow_ready.at[narrow_at[apart]], 1)
            narrow_copy(chunk, apart).start()
        part = pl.ds(2 * starts[chunk], 2 * sizes[chunk])
        narrow_in[narrow_me, part] = narrow_out[narrow_me, part]

    def third_stage(chunk):
        first, count = starts[chunk], sizes[chunk]
        await_narrow(chunk, narrow_recv)
        whole = jnp.concatenate(
            [narrow_in[m, 2 * first : 2 * (first + count)] for m in range(n_narrow)], axis=1
        )
        both = run(jnp.concatenate(split(whole), axis=0), 2)
        final[0, first : first + count] = both[:count]
        final[1, first : first + count] = both[count:]

    qubits_copy.wait()
    swap_copy.wait()
    state_copy.wait()
    gate_copies[0].wait()
    wide_layout = swap_layout(range(upper))
    narrow_layout = swap_layout(list(range(narrow_bits, upper)) + list(range(narrow_bits)))
    prepare(0, natural, wide_layout)
    for plane in range(2):
        high, low = split(state_v[pl.ds(plane, rows, stride=2), :].T)
        turned[plane] = high
        turned[2 + plane] = low
    for chunk in chunks:
        first_stage(chunk)
        first_send(chunk)

    gate_copies[1].wait()
    prepare(1, wide_layout, narrow_layout)
    prepare(2, narrow_layout, natural)

    last = len(sizes) - 1
    for chunk in chunks:
        second_stage(chunk)
        second_send(chunk)
        if chunk > 0:
            third_stage(chunk - 1)
    third_stage(last)

    whole = final[...]
    high, low = whole.max(axis=0), -whole.min(axis=0)
    for k, value in enumerate((high, low)):
        value = value.max(axis=0, keepdims=True)
        ext_out[k : k + 1] = functools.reduce(
            jnp.maximum, [value[:, m * LANES : (m + 1) * LANES] for m in range(tiles)]
        )
    for apart in others:
        ext_copy(apart).start()

    def weave(plane, _):
        out_ref[pl.ds(plane, rows, stride=2), :] = final[plane].T

    lax.fori_loop(0, 2, weave, None)
    for chunk in chunks:
        await_wide(chunk, wide_send)
        await_narrow(chunk, narrow_send)

    await_ext(ext_recv)
    total = jnp.maximum(ext_out[...], ext_in[...].max(axis=0))
    total = jnp.max(total, axis=1, keepdims=True)
    highest, lowest = total[0:1], -total[1:2]
    middle = (highest + lowest) * 0.5
    halfwidth = (highest - lowest) * 0.5 + 1e-06
    middle_ref[...] = jnp.broadcast_to(middle, (1, LANES))
    scale_ref[...] = jnp.broadcast_to(companding / halfwidth, (1, LANES))
    await_ext(ext_send)


def local(state, gates, gate_qubits, swap_order):
    n_wide = lax.axis_size("wide")
    n_narrow = lax.axis_size("narrow")
    upper = state.shape[1].bit_length() - 1 - LANE_QUBITS
    rows = 2**upper
    gate_count, gate_bits = gate_qubits.shape
    gate_dim = 2**gate_bits
    devices = n_wide * n_narrow
    if 2 * rows != n_wide * LANES or rows != n_narrow * LANES or gate_dim != LANES:
        return plain_local(state, gates, gate_qubits, swap_order)
    stages = (range(3), range(3, 6), range(6, gate_count))
    dma = pltpu.SemaphoreType.DMA
    bf16, f32 = jnp.bfloat16, jnp.float32
    sizes = [cut * LANES // sum(CUTS) for cut in CUTS]
    chunks = len(sizes)
    woven = state.reshape(2, rows, LANES).transpose(1, 0, 2).reshape(2 * rows, LANES)
    held = [
        pltpu.with_memory_space_constraint(x, pltpu.HBM)
        for x in (gate_qubits, swap_order, woven, gates)
    ]
    final, middle, scale = pl.pallas_call(
        functools.partial(kernel, n_wide, n_narrow, upper, gate_bits, stages, sizes),
        out_shape=(
            pltpu.VMEM((2 * rows, LANES), f32),
            pltpu.VMEM((1, LANES), f32),
            pltpu.VMEM((1, LANES), f32),
        ),
        in_specs=[pl.BlockSpec(memory_space=pltpu.HBM)] * 4,
        out_specs=[pl.BlockSpec(memory_space=pltpu.VMEM)] * 3,
        scratch_shapes=[
            pltpu.SMEM(gate_qubits.shape, jnp.int32),
            pltpu.SMEM(swap_order.shape, jnp.int32),
            pltpu.VMEM((2 * rows, LANES), f32),
            pltpu.VMEM(gates.shape, f32),
            pltpu.VMEM((gate_count + 3, rows, rows), bf16),
            pltpu.VMEM((gate_count, 4 * gate_dim, 2 * gate_dim), bf16),
            pltpu.VMEM((4, LANES, rows), bf16),
            pltpu.VMEM((n_wide, LANES, LANES), f32),
            pltpu.VMEM((n_wide, LANES, LANES), f32),
            pltpu.VMEM((n_narrow, 2 * LANES, LANES), f32),
            pltpu.VMEM((n_narrow, 2 * LANES, LANES), f32),
            pltpu.VMEM((2, LANES, rows), f32),
            pltpu.VMEM((2, LANES), f32),
            pltpu.VMEM((devices - 1, 2, LANES), f32),
            dma((5,)),
            dma((chunks,)),
            dma((chunks,)),
            dma((chunks,)),
            dma((chunks,)),
            dma((1,)),
            dma((1,)),
            pltpu.SemaphoreType.REGULAR((n_wide,)),
            pltpu.SemaphoreType.REGULAR((n_narrow,)),
        ],
        compiler_params=pltpu.CompilerParams(
            collective_id=0, has_side_effects=True, vmem_limit_bytes=40000000
        ),
        name="gate_layers",
    )(*held)
    values = (final - middle) * scale
    magnitude = jnp.abs(values)
    squared = magnitude * magnitude + 1.0
    grown = jnp.log(magnitude + squared * lax.rsqrt(squared)) * (1.0 / companding_norm)
    final = jnp.where(values < 0, -grown, grown)
    return final.reshape(rows, 2, LANES).transpose(1, 0, 2).reshape(state.shape)


def solution(mesh):
    in_specs = (P(None, ("wide", "narrow")), P(), P(), P())
    out_specs = P(None, ("wide", "narrow"))
    return jax.shard_map(local, mesh=mesh, in_specs=in_specs, out_specs=out_specs, check_vma=False)
```

```python
import functools
import math

import jax
import jax.numpy as jnp
from jax import lax
from jax.experimental import pallas as pl
from jax.experimental.pallas import tpu as pltpu
from jax.sharding import PartitionSpec as P

LANE_QUBITS = 7
LANES = 2**LANE_QUBITS
CHUNKS = 2

companding = 16.0
companding_norm = math.log(16.0 + math.sqrt(257.0))

MESH = pl.DeviceIdType.MESH


def plain_kernel(
    n_wide,
    n_narrow,
    upper,
    gate_bits,
    stages,
    qubits_hbm,
    swap_hbm,
    state_ref,
    gates_ref,
    out_ref,
    qubits_ref,
    swap_ref,
    state_v,
    gates_v,
    perms,
    mats,
    wide_out,
    wide_in,
    narrow_out,
    narrow_in,
    ext_out,
    ext_in,
    local_sem,
    gate_sem,
    wide_send,
    wide_recv,
    narrow_send,
    narrow_recv,
    ext_send,
    ext_recv,
):
    rows = 2**upper
    gate_dim = 2**gate_bits
    rest = rows // gate_dim
    wide_bits = n_wide.bit_length() - 1
    narrow_bits = n_narrow.bit_length() - 1
    wide_me = lax.axis_index("wide")
    narrow_me = lax.axis_index("narrow")
    half = LANES // 2

    qubits_copy = pltpu.make_async_copy(qubits_hbm, qubits_ref, local_sem.at[1])
    qubits_copy.start()
    swap_copy = pltpu.make_async_copy(swap_hbm, swap_ref, local_sem.at[2])
    swap_copy.start()
    state_copy = pltpu.make_async_copy(state_ref, state_v, local_sem.at[0])
    state_copy.start()
    gate_copies = []
    for number in range(gates_v.shape[0]):
        copy = pltpu.make_async_copy(
            gates_ref.at[number], gates_v.at[number], gate_sem.at[number]
        )
        copy.start()
        gate_copies.append(copy)

    barrier = pltpu.get_barrier_semaphore()
    devices = n_wide * n_narrow
    flat_me = wide_me * n_narrow + narrow_me

    def device_at(apart):
        other = lax.rem(flat_me + apart, devices)
        return (lax.div(other, n_narrow), lax.rem(other, n_narrow))

    def for_others(step):
        if devices <= 64:
            for apart in range(1, devices):
                step(apart)
        else:
            lax.fori_loop(1, devices, lambda apart, _: step(apart), None)

    def greet(apart):
        pl.semaphore_signal(barrier, inc=1, device_id=device_at(apart), device_id_type=MESH)

    for_others(greet)
    qubits_copy.wait()
    swap_copy.wait()

    def gate_layout(number):
        masks = [jnp.int32(1) << (qubits_ref[number, k] - LANE_QUBITS) for k in range(gate_bits)]
        left = jnp.int32(rows - 1)
        for mask in masks:
            left = left - mask
        for _ in range(upper - gate_bits):
            low = left & (-left)
            masks.append(low)
            left = left - low
        return masks

    def swap_layout(order):
        return [jnp.int32(1) << (swap_ref[k] - LANE_QUBITS) for k in order]

    natural = [jnp.int32(1 << k) for k in range(upper)]
    wide_layout = swap_layout(range(upper))
    narrow_layout = swap_layout(list(range(narrow_bits, upper)) + list(range(narrow_bits)))

    column = lax.broadcasted_iota(jnp.int32, (1, rows), 1)
    row = lax.broadcasted_iota(jnp.int32, (rows, rows), 0)

    def make_perm(slot, source, target):
        index = jnp.zeros((1, rows), jnp.int32)
        for k in range(upper):
            index = index + jnp.where((column & (1 << k)) != 0, source[k], 0)
        goal = jnp.zeros((1, rows), jnp.int32)
        for k in range(upper):
            goal = goal + jnp.where((index & target[k]) != 0, 1 << k, 0)
        perms[slot] = (row == goal).astype(jnp.float32).astype(jnp.bfloat16)

    def make_matrix(number):
        gate_copies[number].wait()
        whole = jnp.concatenate([gates_v[number, 0], gates_v[number, 1]], axis=1)
        high = whole.astype(jnp.bfloat16)
        low = (whole - high.astype(jnp.float32)).astype(jnp.bfloat16)
        mats[number, :gate_dim] = high
        mats[number, gate_dim:] = low

    sign = jnp.where(lax.broadcasted_iota(jnp.int32, (1, LANES), 1) < half, -1.0, 1.0)

    def permuted(values, slot):
        high = values.astype(jnp.bfloat16)
        low = (values - high.astype(jnp.float32)).astype(jnp.bfloat16)
        both = jnp.concatenate([high, low], axis=1)
        moved = jnp.dot(perms[slot], both, preferred_element_type=jnp.float32)
        return moved[:, :LANES], moved[:, LANES:]

    def gate(values, slot, number):
        both = jnp.concatenate(permuted(values, slot), axis=1)
        blocks = []
        for k in range(rest):
            part = both[k * gate_dim : (k + 1) * gate_dim]
            turned = jnp.concatenate(
                [
                    pltpu.roll(part[:, :LANES], half, 1) * sign,
                    pltpu.roll(part[:, LANES:], half, 1) * sign,
                ],
                axis=1,
            )
            whole = jnp.concatenate([part, turned], axis=0).astype(jnp.bfloat16)
            mixed = jnp.dot(mats[number], whole, preferred_element_type=jnp.float32)
            blocks.append(
                mixed[:gate_dim, :LANES]
                + (mixed[gate_dim:, :LANES] + mixed[:gate_dim, LANES:])
            )
        return jnp.concatenate(blocks, axis=0)

    def moved(values, slot):
        high, low = permuted(values, slot)
        return high + low

    def wide_copy(chunk, apart):
        other = lax.rem(wide_me + apart, n_wide)
        return pltpu.make_async_remote_copy(
            src_ref=wide_out.at[chunk, other],
            dst_ref=wide_in.at[chunk, wide_me],
            send_sem=wide_send.at[chunk, apart - 1],
            recv_sem=wide_recv.at[chunk, apart - 1],
            device_id=(other, narrow_me),
            device_id_type=MESH,
        )

    def narrow_copy(chunk, apart):
        other = lax.rem(narrow_me + apart, n_narrow)
        return pltpu.make_async_remote_copy(
            src_ref=narrow_out.at[chunk, other],
            dst_ref=narrow_in.at[chunk, narrow_me],
            send_sem=narrow_send.at[chunk, apart - 1],
            recv_sem=narrow_recv.at[chunk, apart - 1],
            device_id=(wide_me, other),
            device_id_type=MESH,
        )

    slot = 0
    plan = []
    for numbers, leave in zip(stages, (wide_layout, narrow_layout, natural)):
        plan.append((slot, numbers, leave))
        slot += len(numbers) + 1

    def prepare(stage, layout):
        start, numbers, leave = plan[stage]
        for k, number in enumerate(numbers):
            target = gate_layout(number)
            make_perm(start + k, layout, target)
            make_matrix(number)
            layout = target
        make_perm(start + len(numbers), layout, leave)

    def run(values, stage):
        start, numbers, _ = plan[stage]
        for k, number in enumerate(numbers):
            values = gate(values, start + k, number)
        return moved(values, start + len(numbers))

    prepare(0, natural)
    state_copy.wait()
    real = state_v[pl.ds(0, rows, stride=2), :]
    imag = state_v[pl.ds(1, rows, stride=2), :]
    first_half = lax.broadcasted_iota(jnp.int32, (1, LANES), 1) < half
    pieces = (
        jnp.where(first_half, real, pltpu.roll(imag, half, 1)),
        jnp.where(first_half, pltpu.roll(real, half, 1), imag),
    )
    for chunk in range(CHUNKS):
        values = run(pieces[chunk], 0)
        wide_out[chunk] = values.reshape(n_wide, rows // n_wide, LANES)
        if chunk == 0:
            pl.semaphore_wait(barrier, devices - 1)
        for apart in range(1, n_wide):
            wide_copy(chunk, apart).start()
        wide_in[chunk, wide_me] = wide_out[chunk, wide_me]

    prepare(1, wide_layout)
    prepare(2, narrow_layout)
    for chunk in range(CHUNKS):
        for apart in range(1, n_wide):
            wide_copy(chunk, apart).wait_recv()
        values = run(wide_in[chunk].reshape(rows, LANES), 1)
        narrow_out[chunk] = values.reshape(n_narrow, rows // n_narrow, LANES)
        for apart in range(1, n_narrow):
            narrow_copy(chunk, apart).start()
        narrow_in[chunk, narrow_me] = narrow_out[chunk, narrow_me]

    results = []
    for chunk in range(CHUNKS):
        for apart in range(1, n_narrow):
            narrow_copy(chunk, apart).wait_recv()
        results.append(run(narrow_in[chunk].reshape(rows, LANES), 2))

    high = jnp.maximum(results[0], results[1]).max(axis=0, keepdims=True)
    low = -jnp.minimum(results[0], results[1]).min(axis=0, keepdims=True)
    high = jnp.maximum(high, pltpu.roll(high, half, 1))
    low = jnp.maximum(low, pltpu.roll(low, half, 1))
    ext_out[...] = jnp.where(first_half, high, low)

    def ext_copy(apart):
        return pltpu.make_async_remote_copy(
            src_ref=ext_out,
            dst_ref=ext_in.at[apart - 1],
            send_sem=ext_send.at[apart - 1],
            recv_sem=ext_recv.at[apart - 1],
            device_id=device_at(apart),
            device_id_type=MESH,
        )

    for_others(lambda apart: ext_copy(apart).start())
    state_v[:rows] = jnp.where(first_half, results[0], pltpu.roll(results[1], half, 1))
    state_v[rows:] = jnp.where(first_half, pltpu.roll(results[0], half, 1), results[1])
    for chunk in range(CHUNKS):
        for apart in range(1, n_wide):
            wide_copy(chunk, apart).wait_send()
        for apart in range(1, n_narrow):
            narrow_copy(chunk, apart).wait_send()
    for_others(lambda apart: ext_copy(apart).wait_recv())
    total = jnp.maximum(ext_out[...], ext_in[...].max(axis=0))
    highest = jnp.max(jnp.where(first_half, total, -jnp.inf), axis=1, keepdims=True)
    lowest = -jnp.max(jnp.where(first_half, -jnp.inf, total), axis=1, keepdims=True)
    middle = (highest + lowest) * 0.5
    halfwidth = (highest - lowest) * 0.5 + 1e-06
    scale = companding / halfwidth
    for plane in range(2):
        values = (state_v[plane * rows : (plane + 1) * rows] - middle) * scale
        magnitude = jnp.abs(values)
        squared = magnitude * magnitude + 1.0
        grown = jnp.log(magnitude + squared * lax.rsqrt(squared)) * (1.0 / companding_norm)
        out_ref[pl.ds(plane, rows, stride=2), :] = jnp.where(values < 0, -grown, grown)
    for_others(lambda apart: ext_copy(apart).wait_send())


def plain_local(state, gates, gate_qubits, swap_order):
    n_wide = lax.axis_size("wide")
    n_narrow = lax.axis_size("narrow")
    upper = state.shape[1].bit_length() - 1 - LANE_QUBITS
    rows = 2**upper
    gate_count, gate_bits = gate_qubits.shape
    gate_dim = 2**gate_bits
    stages = (range(3), range(3, 6), range(6, gate_count))
    dma = pltpu.SemaphoreType.DMA
    woven = state.reshape(2, rows, LANES).transpose(1, 0, 2).reshape(2 * rows, LANES)
    final = pl.pallas_call(
        functools.partial(plain_kernel, n_wide, n_narrow, upper, gate_bits, stages),
        out_shape=jax.ShapeDtypeStruct((2 * rows, LANES), jnp.float32),
        in_specs=[pl.BlockSpec(memory_space=pltpu.HBM)] * 4,
        out_specs=pl.BlockSpec(memory_space=pltpu.VMEM),
        scratch_shapes=[
            pltpu.SMEM(gate_qubits.shape, jnp.int32),
            pltpu.SMEM(swap_order.shape, jnp.int32),
            pltpu.VMEM((2 * rows, LANES), jnp.float32),
            pltpu.VMEM(gates.shape, jnp.float32),
            pltpu.VMEM((gate_count + 3, rows, rows), jnp.bfloat16),
            pltpu.VMEM((gate_count, 2 * gate_dim, 2 * gate_dim), jnp.bfloat16),
            pltpu.VMEM((CHUNKS, n_wide, rows // n_wide, LANES), jnp.float32),
            pltpu.VMEM((CHUNKS, n_wide, rows // n_wide, LANES), jnp.float32),
            pltpu.VMEM((CHUNKS, n_narrow, rows // n_narrow, LANES), jnp.float32),
            pltpu.VMEM((CHUNKS, n_narrow, rows // n_narrow, LANES), jnp.float32),
            pltpu.VMEM((1, LANES), jnp.float32),
            pltpu.VMEM((n_wide * n_narrow - 1, 1, LANES), jnp.float32),
            dma((3,)),
            dma((gate_count,)),
            dma((CHUNKS, n_wide - 1)),
            dma((CHUNKS, n_wide - 1)),
            dma((CHUNKS, n_narrow - 1)),
            dma((CHUNKS, n_narrow - 1)),
            dma((n_wide * n_narrow - 1,)),
            dma((n_wide * n_narrow - 1,)),
        ],
        compiler_params=pltpu.CompilerParams(
            collective_id=0, has_side_effects=True, vmem_limit_bytes=67043328
        ),
        name="plain_gate_layers",
    )(gate_qubits, swap_order, woven, gates)
    return final.reshape(rows, 2, LANES).transpose(1, 0, 2).reshape(state.shape)


CUTS = (64, 64)


def kernel(
    n_wide,
    n_narrow,
    upper,
    gate_bits,
    stages,
    sizes,
    qubits_hbm,
    swap_hbm,
    state_ref,
    gates_ref,
    out_ref,
    middle_ref,
    scale_ref,
    qubits_ref,
    swap_ref,
    state_v,
    gates_v,
    perms,
    mats,
    turned,
    wide_out,
    wide_in,
    narrow_out,
    narrow_in,
    final,
    ext_out,
    ext_in,
    local_sem,
    wide_send,
    wide_recv,
    narrow_send,
    narrow_recv,
    ext_send,
    ext_recv,
    wide_ready,
    narrow_ready,
):
    rows = 2**upper
    gate_dim = 2**gate_bits
    rest = rows // gate_dim
    tiles = rows // LANES
    narrow_bits = n_narrow.bit_length() - 1
    wide_me = lax.axis_index("wide")
    narrow_me = lax.axis_index("narrow")
    half = LANES // 2
    chunks = range(len(sizes))
    starts = [sum(sizes[:k]) for k in chunks]
    devices = n_wide * n_narrow
    f32, bf16 = jnp.float32, jnp.bfloat16

    qubits_copy = pltpu.make_async_copy(qubits_hbm, qubits_ref, local_sem.at[1])
    qubits_copy.start()
    swap_copy = pltpu.make_async_copy(swap_hbm, swap_ref, local_sem.at[2])
    swap_copy.start()
    state_copy = pltpu.make_async_copy(state_ref, state_v, local_sem.at[0])
    state_copy.start()
    soon = len(stages[0])
    gate_copies = [
        pltpu.make_async_copy(
            gates_ref.at[first:after], gates_v.at[first:after], local_sem.at[3 + k]
        )
        for k, (first, after) in enumerate(((0, soon), (soon, gates_v.shape[0])))
    ]
    for copy in gate_copies:
        copy.start()

    barrier = pltpu.get_barrier_semaphore()

    def partners(me, count):
        found = [me]
        for k in range(count.bit_length() - 1):
            step = (1 << k) * (1 - 2 * lax.rem(lax.div(me, 1 << k), 2))
            found = found + [other + step for other in found]
        return found

    wide_at = partners(wide_me, n_wide)
    narrow_at = partners(narrow_me, n_narrow)
    flat_me = wide_me * n_narrow + narrow_me

    def greet_wide(other, _):
        pl.semaphore_signal(
            barrier, inc=1, device_id=(other, narrow_me), device_id_type=MESH
        )

    def greet_narrow(other, _):
        pl.semaphore_signal(barrier, inc=1, device_id=(wide_me, other), device_id_type=MESH)

    lax.fori_loop(wide_me + 1, n_wide, greet_wide, None)
    lax.fori_loop(narrow_me + 1, n_narrow, greet_narrow, None)

    def answer_wide(other, _):
        pl.semaphore_signal(
            wide_ready.at[wide_me], inc=1, device_id=(other, narrow_me), device_id_type=MESH
        )
        pl.semaphore_signal(wide_ready.at[other], inc=1)

    def answer_narrow(other, _):
        pl.semaphore_signal(
            narrow_ready.at[narrow_me], inc=1, device_id=(wide_me, other), device_id_type=MESH
        )
        pl.semaphore_signal(narrow_ready.at[other], inc=1)


    @pl.when(wide_me + narrow_me > 0)
    def _():
        pl.semaphore_wait(barrier, wide_me + narrow_me)

    lax.fori_loop(0, wide_me, answer_wide, None)
    lax.fori_loop(0, narrow_me, answer_narrow, None)

    def gate_layout(number):
        masks = [jnp.int32(1) << (qubits_ref[number, k] - LANE_QUBITS) for k in range(gate_bits)]
        left = jnp.int32(rows - 1)
        for mask in masks:
            left = left - mask
        for _ in range(upper - gate_bits):
            low = left & (-left)
            masks.append(low)
            left = left - low
        return masks

    def swap_layout(order):
        return [jnp.int32(1) << (swap_ref[k] - LANE_QUBITS) for k in order]

    natural = [jnp.int32(1 << k) for k in range(upper)]
    column = lax.broadcasted_iota(jnp.int32, (1, rows), 1)
    row = lax.broadcasted_iota(jnp.int32, (rows, rows), 0).astype(jnp.int16)
    first_half = lax.broadcasted_iota(jnp.int32, (1, LANES), 1) < half

    def make_perm(slot, source, target):
        index = jnp.zeros((1, rows), jnp.int32)
        for k in range(upper):
            index = index + jnp.where((column & (1 << k)) != 0, target[k], 0)
        place = jnp.zeros((1, rows), jnp.int32)
        for k in range(upper):
            place = place + jnp.where((index & source[k]) != 0, 1 << k, 0)
        perms[slot] = jnp.where(row == place.astype(jnp.int16), bf16(1), bf16(0))

    def split(values):
        high = values.astype(bf16)
        return high, (values - high.astype(f32)).astype(bf16)

    def make_matrix(number):
        real = split(gates_v[number, 0].T)
        imag = split(gates_v[number, 1].T)
        for k in range(2):
            top, bottom = 2 * k * gate_dim, (2 * k + 1) * gate_dim
            mats[number, top:bottom, :gate_dim] = real[k]
            mats[number, top:bottom, gate_dim:] = imag[k]
            mats[number, bottom : bottom + gate_dim, :gate_dim] = -imag[k]
            mats[number, bottom : bottom + gate_dim, gate_dim:] = real[k]

    def moved(parts, slot):
        middle = rows // 2
        return jnp.concatenate(
            [
                jnp.dot(parts, perms[slot, :, :middle], preferred_element_type=f32),
                jnp.dot(parts, perms[slot, :, middle:], preferred_element_type=f32),
            ],
            axis=1,
        )

    def gate(parts, slot, number):
        count = parts.shape[0] // 4
        parts = moved(parts, slot).astype(bf16)

        def side(first):
            return jnp.concatenate(
                [
                    jnp.concatenate(
                        [
                            parts[first : first + count, k * gate_dim : (k + 1) * gate_dim],
                            parts[first + count : first + 2 * count, k * gate_dim : (k + 1) * gate_dim],
                        ],
                        axis=1,
                    )
                    for k in range(rest)
                ],
                axis=0,
            )

        high, low = side(0), side(2 * count)
        weights = jnp.concatenate([mats[number, : 2 * gate_dim], mats[number]], axis=0)
        whole = jnp.concatenate([high, low, high], axis=1)
        middle = whole.shape[0] // 2
        mixed = jnp.concatenate(
            [
                jnp.dot(whole[:middle], weights, preferred_element_type=f32),
                jnp.dot(whole[middle:], weights, preferred_element_type=f32),
            ],
            axis=0,
        )
        return jnp.concatenate(
            [
                jnp.concatenate(
                    [
                        part[k * count : (k + 1) * count, plane * gate_dim : (plane + 1) * gate_dim]
                        for k in range(rest)
                    ],
                    axis=1,
                )
                for part in split(mixed)
                for plane in range(2)
            ],
            axis=0,
        )

    slot = 0
    plan = []
    for numbers in stages:
        plan.append((slot, numbers))
        slot += len(numbers) + 1

    def prepare(stage, layout, leave):
        start, numbers = plan[stage]
        for k, number in enumerate(numbers):
            target = gate_layout(number)
            make_perm(start + k, layout, target)
            make_matrix(number)
            layout = target
        make_perm(start + len(numbers), layout, leave)

    def run(parts, stage):
        start, numbers = plan[stage]
        for k, number in enumerate(numbers):
            parts = gate(parts, start + k, number)
        both = moved(parts, start + len(numbers))
        count = both.shape[0] // 2
        return both[:count] + both[count:]

    def wide_copy(chunk, apart):
        other = wide_at[apart]
        part = pl.ds(starts[chunk], sizes[chunk])
        return pltpu.make_async_remote_copy(
            src_ref=wide_out.at[other, part],
            dst_ref=wide_in.at[wide_me, part],
            send_sem=wide_send.at[chunk],
            recv_sem=wide_recv.at[chunk],
            device_id=(other, narrow_me),
            device_id_type=MESH,
        )

    def narrow_copy(chunk, apart):
        other = narrow_at[apart]
        part = pl.ds(2 * starts[chunk], 2 * sizes[chunk])
        return pltpu.make_async_remote_copy(
            src_ref=narrow_out.at[other, part],
            dst_ref=narrow_in.at[narrow_me, part],
            send_sem=narrow_send.at[chunk],
            recv_sem=narrow_recv.at[chunk],
            device_id=(wide_me, other),
            device_id_type=MESH,
        )

    def ext_copy(place):
        other = place + lax.div(place + devices - flat_me, devices)
        return pltpu.make_async_remote_copy(
            src_ref=ext_out,
            dst_ref=ext_in.at[flat_me],
            send_sem=ext_send.at[0],
            recv_sem=ext_recv.at[0],
            device_id=(lax.div(other, n_narrow), lax.rem(other, n_narrow)),
            device_id_type=MESH,
        )

    def await_wide(chunk, sems):
        all_of = wide_in.at[: n_wide - 1, pl.ds(starts[chunk], sizes[chunk])]
        pltpu.make_async_copy(all_of, all_of, sems.at[chunk]).wait()

    def await_narrow(chunk, sems):
        all_of = narrow_in.at[: n_narrow - 1, pl.ds(2 * starts[chunk], 2 * sizes[chunk])]
        pltpu.make_async_copy(all_of, all_of, sems.at[chunk]).wait()

    def await_ext(sems):
        all_of = ext_in.at[: devices - 1]
        pltpu.make_async_copy(all_of, all_of, sems.at[0]).wait()

    def first_stage(chunk):
        first, count = starts[chunk], sizes[chunk]
        parts = jnp.concatenate(
            [turned[k, first : first + count] for k in range(4)], axis=0
        )
        both = run(parts, 0)
        real, imag = both[:count], both[count:]
        for m in range(tiles):
            re, im = real[:, m * LANES : (m + 1) * LANES], imag[:, m * LANES : (m + 1) * LANES]
            wide_out[2 * m, first : first + count] = jnp.where(
                first_half, re, pltpu.roll(im, half, 1)
            )
            wide_out[2 * m + 1, first : first + count] = jnp.where(
                first_half, pltpu.roll(re, half, 1), im
            )

    def first_send(chunk):
        for apart in range(1, n_wide):
            if chunk == 0:
                pl.semaphore_wait(wide_ready.at[wide_at[apart]], 1)
            wide_copy(chunk, apart).start()
        part = pl.ds(starts[chunk], sizes[chunk])
        wide_in[wide_me, part] = wide_out[wide_me, part]

    def second_stage(chunk):
        first, count = starts[chunk], sizes[chunk]
        await_wide(chunk, wide_recv)
        real, imag = [], []
        for m in range(tiles):
            left = wide_in[2 * m, first : first + count]
            right = wide_in[2 * m + 1, first : first + count]
            real.append(jnp.where(first_half, left, pltpu.roll(right, half, 1)))
            imag.append(jnp.where(first_half, pltpu.roll(left, half, 1), right))
        whole = jnp.concatenate(
            [jnp.concatenate(real, axis=1), jnp.concatenate(imag, axis=1)], axis=0
        )
        both = run(jnp.concatenate(split(whole), axis=0), 1)
        width = rows // n_narrow
        for m in range(n_narrow):
            narrow_out[m, 2 * first : 2 * (first + count)] = both[:, m * width : (m + 1) * width]

    def second_send(chunk):
        for apart in range(1, n_narrow):
            if chunk == 0:
                pl.semaphore_wait(narrow_ready.at[narrow_at[apart]], 1)
            narrow_copy(chunk, apart).start()
        part = pl.ds(2 * starts[chunk], 2 * sizes[chunk])
        narrow_in[narrow_me, part] = narrow_out[narrow_me, part]

    def third_stage(chunk):
        first, count = starts[chunk], sizes[chunk]
        await_narrow(chunk, narrow_recv)
        whole = jnp.concatenate(
            [narrow_in[m, 2 * first : 2 * (first + count)] for m in range(n_narrow)], axis=1
        )
        both = run(jnp.concatenate(split(whole), axis=0), 2)
        final[0, first : first + count] = both[:count]
        final[1, first : first + count] = both[count:]

    qubits_copy.wait()
    swap_copy.wait()
    state_copy.wait()
    gate_copies[0].wait()
    wide_layout = swap_layout(range(upper))
    narrow_layout = swap_layout(list(range(narrow_bits, upper)) + list(range(narrow_bits)))
    prepare(0, natural, wide_layout)
    for plane in range(2):
        high, low = split(state_v[pl.ds(plane, rows, stride=2), :].T)
        turned[plane] = high
        turned[2 + plane] = low
    for chunk in chunks:
        first_stage(chunk)
        first_send(chunk)

    gate_copies[1].wait()
    prepare(1, wide_layout, narrow_layout)
    prepare(2, narrow_layout, natural)

    last = len(sizes) - 1
    for chunk in chunks:
        second_stage(chunk)
        second_send(chunk)
        if chunk > 0:
            third_stage(chunk - 1)
    third_stage(last)

    whole = final[...]
    high, low = whole.max(axis=0), -whole.min(axis=0)
    for k, value in enumerate((high, low)):
        value = value.max(axis=0, keepdims=True)
        ext_out[k : k + 1] = functools.reduce(
            jnp.maximum, [value[:, m * LANES : (m + 1) * LANES] for m in range(tiles)]
        )
    for place in range(devices - 1):
        ext_copy(place).start()
    ext_in[flat_me] = ext_out[...]

    def weave(plane, _):
        out_ref[pl.ds(plane, rows, stride=2), :] = final[plane].T

    lax.fori_loop(0, 2, weave, None)
    for chunk in chunks:
        await_wide(chunk, wide_send)
        await_narrow(chunk, narrow_send)

    await_ext(ext_recv)
    total = ext_in[...].max(axis=0)
    total = jnp.max(total, axis=1, keepdims=True)
    highest, lowest = total[0:1], -total[1:2]
    middle = (highest + lowest) * 0.5
    halfwidth = (highest - lowest) * 0.5 + 1e-06
    middle_ref[...] = jnp.broadcast_to(middle, (1, LANES))
    scale_ref[...] = jnp.broadcast_to(companding / halfwidth, (1, LANES))
    await_ext(ext_send)


def local(state, gates, gate_qubits, swap_order):
    n_wide = lax.axis_size("wide")
    n_narrow = lax.axis_size("narrow")
    upper = state.shape[1].bit_length() - 1 - LANE_QUBITS
    rows = 2**upper
    gate_count, gate_bits = gate_qubits.shape
    gate_dim = 2**gate_bits
    devices = n_wide * n_narrow
    if 2 * rows != n_wide * LANES or rows != n_narrow * LANES or gate_dim != LANES:
        return plain_local(state, gates, gate_qubits, swap_order)
    stages = (range(3), range(3, 6), range(6, gate_count))
    dma = pltpu.SemaphoreType.DMA
    bf16, f32 = jnp.bfloat16, jnp.float32
    sizes = [cut * LANES // sum(CUTS) for cut in CUTS]
    chunks = len(sizes)
    woven = state.reshape(2, rows, LANES).transpose(1, 0, 2).reshape(2 * rows, LANES)
    held = [
        pltpu.with_memory_space_constraint(x, pltpu.HBM)
        for x in (gate_qubits, swap_order, woven, gates)
    ]
    final, middle, scale = pl.pallas_call(
        functools.partial(kernel, n_wide, n_narrow, upper, gate_bits, stages, sizes),
        out_shape=(
            pltpu.VMEM((2 * rows, LANES), f32),
            pltpu.VMEM((1, LANES), f32),
            pltpu.VMEM((1, LANES), f32),
        ),
        in_specs=[pl.BlockSpec(memory_space=pltpu.HBM)] * 4,
        out_specs=[pl.BlockSpec(memory_space=pltpu.VMEM)] * 3,
        scratch_shapes=[
            pltpu.SMEM(gate_qubits.shape, jnp.int32),
            pltpu.SMEM(swap_order.shape, jnp.int32),
            pltpu.VMEM((2 * rows, LANES), f32),
            pltpu.VMEM(gates.shape, f32),
            pltpu.VMEM((gate_count + 3, rows, rows), bf16),
            pltpu.VMEM((gate_count, 4 * gate_dim, 2 * gate_dim), bf16),
            pltpu.VMEM((4, LANES, rows), bf16),
            pltpu.VMEM((n_wide, LANES, LANES), f32),
            pltpu.VMEM((n_wide, LANES, LANES), f32),
            pltpu.VMEM((n_narrow, 2 * LANES, LANES), f32),
            pltpu.VMEM((n_narrow, 2 * LANES, LANES), f32),
            pltpu.VMEM((2, LANES, rows), f32),
            pltpu.VMEM((2, LANES), f32),
            pltpu.VMEM((devices, 2, LANES), f32),
            dma((5,)),
            dma((chunks,)),
            dma((chunks,)),
            dma((chunks,)),
            dma((chunks,)),
            dma((1,)),
            dma((1,)),
            pltpu.SemaphoreType.REGULAR((n_wide,)),
            pltpu.SemaphoreType.REGULAR((n_narrow,)),
        ],
        compiler_params=pltpu.CompilerParams(
            collective_id=0, has_side_effects=True, vmem_limit_bytes=40000000
        ),
        name="gate_layers",
    )(*held)
    values = (final - middle) * scale
    magnitude = jnp.abs(values)
    squared = magnitude * magnitude + 1.0
    grown = jnp.log(magnitude + squared * lax.rsqrt(squared)) * (1.0 / companding_norm)
    final = jnp.where(values < 0, -grown, grown)
    return final.reshape(rows, 2, LANES).transpose(1, 0, 2).reshape(state.shape)


def solution(mesh):
    in_specs = (P(None, ("wide", "narrow")), P(), P(), P())
    out_specs = P(None, ("wide", "narrow"))
    return jax.shard_map(local, mesh=mesh, in_specs=in_specs, out_specs=out_specs, check_vma=False)
```
